32 devices in a mesh: dp: 16 (over z, y, x), tensor: 2 (over core).
Axes of the slice: x: 2, y: 2, z: 4, core: 2. Of those that a mesh axis runs over, the one named last changes fastest.
Arguments:
- tokens: bfloat16 [32, 1024, 640], P(('dp', 'tensor')), may hold values from -6 to 6
- out_grad: bfloat16 [32, 1024, 640], P(('dp', 'tensor')), may hold values from -6 to 6
- segment_ids: int32 [32, 1024], P('dp'), may hold values from 0 to 7, never falling along the last dimension, each value on 1 to 512 neighbouring positions
- token_live: int32 [32, 1024], P('dp'), may hold values from 0 to 1, as said below
- live_rows: int32 [16], P('dp'), may hold values from 1 to 2, as said below
- targets: int32 [32, 1024], P(('dp', 'tensor')), may hold values from -33 to 32
- predicted: int32 [32, 1024], P(('dp', 'tensor')), may hold values from 0 to 32
- w_qkv: bfloat16 [3, 640, 640], P(None, None, 'tensor'), may hold values from -0.25 to 0.25
- b_qkv: bfloat16 [3, 640], P(None, 'tensor'), may hold values from -3 to 3
- w_out: bfloat16 [640, 640], P('tensor'), may hold values from -1.25 to 1.25
- b_out: bfloat16 [640], replicated, may hold values from -2 to 2
- norm1_gain: bfloat16 [640], replicated, may hold values from 0.099609375 to 1.8984375
- norm1_bias: bfloat16 [640], replicated, may hold values from -2 to 2
- norm2_gain: bfloat16 [640], replicated, may hold values from 0.099609375 to 1.8984375
- norm2_bias: bfloat16 [640], replicated, may hold values from -2 to 2
- w_up: bfloat16 [640, 2560], P(None, 'tensor'), may hold values from -0.25 to 0.25
- b_up: bfloat16 [2560], P('tensor'), may hold values from -3 to 3
- w_down: bfloat16 [2560, 640], P('tensor'), may hold values from -0.125 to 0.125
- b_down: bfloat16 [640], replicated, may hold values from -2 to 2
Outputs:
- out_act: bfloat16 [32, 1024, 640], P(('dp', 'tensor'))
- in_grad: bfloat16 [32, 1024, 640], P(('dp', 'tensor'))
- grad_w_qkv: float32 [3, 640, 640], P(None, None, 'tensor')
- grad_b_qkv: float32 [3, 640], P(None, 'tensor')
- grad_w_out: float32 [640, 640], P('tensor')
- grad_b_out: float32 [640], replicated
- grad_norm1_gain: float32 [640], replicated
- grad_norm1_bias: float32 [640], replicated
- grad_norm2_gain: float32 [640], replicated
- grad_norm2_bias: float32 [640], replicated
- grad_w_up: float32 [640, 2560], P(None, 'tensor')
- grad_b_up: float32 [2560], P('tensor')
- grad_w_down: float32 [2560, 640], P('tensor')
- grad_b_down: float32 [640], replicated
- counts: int32 [3], replicated
- row_correct: int32 [32], P(('dp', 'tensor'))
The draws below stay inside these ranges and needn't reach their ends.
Inputs may be any that keep to these rules, and one draw needn't show every extreme that they name: `token_live`: each row's live tokens are a prefix of 512 or more positions. `live_rows`: slots below this count in a data index hold proteins; the rest of its 2 slots are padding. Some data index is full in every draw. `segment_ids`: never falling along a row. `targets`: A negative value marks a position that is not masked.
All inputs are finite; a program needn't handle non-finite values.
Results may differ from the reference program's by a relative error of at most 0.012.
The reference program's roundings to bfloat16 on the way count: a program that leaves them out, or rounds other values in their place, can miss the bound.
Values may be sent and summed in bfloat16 or wider, within the bound.
No kernel may reach another device: no remote copies, remote signals or barrier semaphores. Data moves between devices by JAX's collectives and lax.ppermute only.
A program may use at most 192 MiB of HBM per device.

```python
import math
import jax
import jax.numpy as jnp
import numpy as np
from jax import lax

D = 640
HEADS = 20
HEAD_DIM = 32
FF = 2560
VOCAB = 33
SEQ = 1024
ROWS_DEV = 2
INNER = 640
GROUPS = 16
ROWS = 32
N_DP = 16


def draw_token_live(key, part):
    lengths = jax.random.randint(key, (ROWS, 1), SEQ // 2, SEQ + 1)
    places = jnp.arange(SEQ, dtype=jnp.int32)[None, :]
    return (places < lengths).astype(jnp.int32)


def draw_live_rows(key, part):
    first, second = jax.random.split(key)
    filled = jax.random.randint(first, (GROUPS,), 1, ROWS_DEV + 1)
    full_at = jax.random.randint(second, (), 0, GROUPS)
    return jnp.where(jnp.arange(GROUPS) == full_at, ROWS_DEV, filled).astype(jnp.int32)


def set_ends(drawn, rng, low, largest):
    longest = drawn.shape.index(max(drawn.shape))
    spots = []
    for shift in (0, 1):
        where = [jax.random.randint(jax.random.fold_in(rng, axis), (), 0, length) for axis, length in enumerate(drawn.shape)]
        where[longest] = (where[longest] + shift) % drawn.shape[longest]
        spots.append(tuple(where))
    return drawn.at[spots[0]].set(low).at[spots[1]].set(largest)


def levels(own_key, extent, cuts, least, largest):
    def one(axis_at, blocks):
        draws = jax.random.uniform(jax.random.fold_in(jax.random.fold_in(own_key, 6), axis_at), (blocks,), jnp.float32, least / len(cuts), largest / len(cuts))
        return jnp.repeat(jnp.exp(draws), extent[axis_at] // blocks).reshape((-1,) + (1,) * (len(extent) - axis_at - 1))

    level = one(*cuts[0])
    for cut in cuts[1:]:
        level = level * one(*cut)
    return level


def length_profile(number_of, total, bound, slope):
    loads = [(1 << 20) // math.isqrt(rank ** slope) + 1 for rank in range(2, number_of + 1)]
    surplus, holding = total - bound - (number_of - 1), [1] * (number_of - 1)
    while surplus > 0:
        free = [i for i in range(number_of - 1) if holding[i] < bound]
        mass, left = sum([loads[i] for i in free]), surplus
        for i in free:
            more = min(bound - holding[i], max(1, left * loads[i] // mass), surplus)
            holding[i] = holding[i] + more
            surplus = surplus - more
    return np.array([bound] + holding)


def uneven_parts(stream_key, number_of, total, reach, lean):
    if number_of == 2:
        one = jax.random.randint(stream_key, (), max(1, total - reach), min(reach, total - 1) + 1)
        return jnp.stack([one, total - one])
    tallies = jnp.asarray(length_profile(number_of, total, reach, lean), jnp.int32)
    twos = (number_of - 1) // 2
    giver, sink = tallies[1:1 + 2 * twos:2], tallies[2:2 + 2 * twos:2]
    slack = jnp.minimum(giver - 1, reach - sink)
    shifted = jax.random.randint(jax.random.fold_in(stream_key, 1), (twos,), 0, 1 << 20) % (slack + 1)
    tallies = tallies.at[1:1 + 2 * twos:2].set(giver - shifted).at[2:2 + 2 * twos:2].set(sink + shifted)
    return tallies[jax.random.permutation(jax.random.fold_in(stream_key, 2), number_of)]


def centred(key, extent, deviation, bound, cuts=(), kind=jnp.bfloat16):
    drawn = deviation * jax.random.normal(key, extent, jnp.float32)
    if cuts:
        drawn = drawn * levels(key, extent, cuts, -0.22, 0.18)
    return jnp.clip(drawn, -bound, bound).astype(kind)


def setup_inputs(seed: int = 0) -> dict:
    key_list = jax.random.split(jax.random.key(seed), 20)
    return {
        "tokens": centred(key_list[0], (ROWS, SEQ, D), 1.0, 6.0, ((0, 32),)),
        "out_grad": centred(key_list[1], (ROWS, SEQ, D), 1.0, 6.0, ((0, 32),)),
        "segment_ids": jax.vmap(lambda own: jnp.searchsorted(jnp.cumsum(uneven_parts(own, 8, SEQ, SEQ // 2, 1)), jnp.arange(SEQ), side="right"))(jax.random.split(key_list[2], ROWS)).reshape((ROWS, SEQ)).astype(jnp.int32),
        "token_live": draw_token_live(jax.random.fold_in(key_list[19], 71), 0),
        "live_rows": draw_live_rows(jax.random.fold_in(key_list[19], 71), 0),
        "targets": set_ends(jax.random.randint(key_list[5], (ROWS, SEQ), -VOCAB, VOCAB), jax.random.fold_in(key_list[5], 1), -VOCAB, VOCAB - 1).astype(jnp.int32),
        "predicted": set_ends(jax.random.randint(key_list[6], (ROWS, SEQ), 0, VOCAB), jax.random.fold_in(key_list[6], 1), 0, VOCAB - 1).astype(jnp.int32),
        "w_qkv": centred(key_list[7], (3, D, INNER), D ** -0.5, 0.25, ((2, 2),)),
        "b_qkv": centred(key_list[8], (3, INNER), 0.5, 3.0, ((1, 2),)),
        "w_out": centred(key_list[9], (INNER, D), (INNER // 32) ** -0.5, 1.25, ((0, 2),)),
        "b_out": centred(key_list[10], (D,), 0.3, 2.0),
        "norm1_gain": jnp.clip(1.0 + 0.18 * jax.random.normal(key_list[11], (D,), jnp.float32), 0.099609375, 1.8984375).astype(jnp.bfloat16),
        "norm1_bias": centred(key_list[12], (D,), 0.3, 2.0),
        "norm2_gain": jnp.clip(1.0 + 0.18 * jax.random.normal(key_list[13], (D,), jnp.float32), 0.099609375, 1.8984375).astype(jnp.bfloat16),
        "norm2_bias": centred(key_list[14], (D,), 0.3, 2.0),
        "w_up": centred(key_list[15], (D, FF), D ** -0.5, 0.25, ((1, 2),)),
        "b_up": centred(key_list[16], (FF,), 0.5, 3.0, ((0, 2),)),
        "w_down": centred(key_list[17], (FF, D), FF ** -0.5, 0.125, ((0, 2),)),
        "b_down": centred(key_list[18], (D,), 0.3, 2.0),
    }


@jax.custom_vjp
def low(v):
    return lax.optimization_barrier(v.astype(jnp.bfloat16)).astype(jnp.float32)

@jax.custom_vjp
def low_back(v):
    return v

def low_keep(v):
    return (low(v), None)

def low_pass(kept, grad):
    return (grad,)

def back_keep(v):
    return (v, None)

def back_low(kept, grad):
    return (low(grad),)
low.defvjp(low_keep, low_pass)
low_back.defvjp(back_keep, back_low)

def layer_norm(values, gain, shift):
    average = lax.optimization_barrier(jnp.mean(values, axis=-1, keepdims=True))
    centered = values - average
    variance = lax.optimization_barrier(jnp.mean(centered * centered, axis=-1, keepdims=True))
    return centered * lax.rsqrt(variance + 1e-05) * gain + shift

def rotary_tables(segments, head_dim):
    length = segments.shape[1]
    places = jnp.arange(length, dtype=jnp.int32)
    earlier = jnp.concatenate([segments[:, :1] - 1, segments[:, :-1]], axis=1)
    starts = jnp.where(segments != earlier, places[None, :], jnp.zeros_like(segments))
    begins = lax.cummax(starts, axis=1)
    offsets = (places[None, :] - begins).astype(jnp.float32)
    half = head_dim // 2
    inverse = jnp.exp(jnp.arange(half, dtype=jnp.float32) * (-2.0 * math.log(10000.0) / head_dim))
    angles = offsets[:, :, None] * inverse[None, None, :]
    angles = jnp.concatenate([angles, angles], axis=-1)
    return (jnp.cos(angles), jnp.sin(angles))

def rotary(values, cosine, sine):
    half = values.shape[-1] // 2
    turned = jnp.concatenate([-values[..., half:], values[..., :half]], axis=-1)
    return values * cosine[:, :, None, :] + turned * sine[:, :, None, :]

def attend_row(pieces):
    query_row, key_row, value_row, segment_row, alive_row = pieces
    length = segment_row.shape[0]
    same = (segment_row[:, None] == segment_row[None, :]) & (alive_row[None, :] > 0)
    allowed = same | jnp.eye(length, dtype=bool)
    scores = low_back(jnp.einsum('qhe,khe->hqk', query_row, key_row, precision=lax.Precision.HIGHEST))
    scores = jnp.where(allowed[None], scores, -1000000000.0)
    weights = low(jax.nn.softmax(scores, axis=-1))
    return jnp.einsum('hqk,khe->qhe', weights, value_row, precision=lax.Precision.HIGHEST)

def forward(params, inputs, segments, alive, cosine, sine):
    w_qkv, b_qkv, w_out, b_out, gain_one, shift_one, gain_two, shift_two, w_up, b_up, w_down, b_down = params
    highest = lax.Precision.HIGHEST
    rows, length = (inputs.shape[0], inputs.shape[1])
    normed = low(layer_norm(inputs, gain_one, shift_one))
    projected = low_back(jnp.einsum('rld,cde->crle', normed, w_qkv, precision=highest)) + b_qkv[:, None, None, :]
    heads_shape = (rows, length, HEADS, HEAD_DIM)
    queries = low(rotary(projected[0].reshape(heads_shape), cosine, sine) * (1.0 / math.sqrt(HEAD_DIM)))
    keys = low(rotary(projected[1].reshape(heads_shape), cosine, sine))
    values = low(projected[2].reshape(heads_shape))
    attended = lax.map(jax.checkpoint(attend_row), (queries, keys, values, segments, alive))
    mixed = low(low_back(attended.reshape(rows, length, INNER)))
    middle = inputs + low_back(jnp.einsum('rle,ed->rld', mixed, w_out, precision=highest)) + b_out
    normed_two = low(layer_norm(middle, gain_two, shift_two))
    hidden = low_back(jnp.einsum('rld,df->rlf', normed_two, w_up, precision=highest)) + b_up
    activated = low(jax.nn.gelu(hidden, approximate=False))
    return middle + low_back(jnp.einsum('rlf,fd->rld', activated, w_down, precision=highest)) + b_down

def grouped(array):
    return array.reshape((N_DP, ROWS_DEV) + array.shape[1:])

def reference(tokens, out_grad, segment_ids, token_live, live_rows, targets, predicted, w_qkv, b_qkv, w_out, b_out, norm1_gain, norm1_bias, norm2_gain, norm2_bias, w_up, b_up, w_down, b_down):
    params = tuple((weight.astype(jnp.float32) for weight in (w_qkv, b_qkv, w_out, b_out, norm1_gain, norm1_bias, norm2_gain, norm2_bias, w_up, b_up, w_down, b_down)))
    slots = jnp.arange(ROWS, dtype=jnp.int32) % ROWS_DEV
    owners = jnp.arange(ROWS, dtype=jnp.int32) // ROWS_DEV
    row_alive = (slots < live_rows[owners]).astype(jnp.int32)
    alive = token_live * row_alive[:, None]
    masked = ((targets >= 0) & (alive > 0)).astype(jnp.int32)

    def group_step(running, pieces):
        inputs, cotangent, segments, alive_group, masked_group = pieces
        cosine, sine = rotary_tables(segments, HEAD_DIM)

        def run(weights, source):
            return forward(weights, source, segments, alive_group, cosine, sine)
        result, pull = jax.vjp(run, params, inputs.astype(jnp.float32))
        weight_grads, input_grads = pull(cotangent.astype(jnp.float32) * masked_group[:, :, None].astype(jnp.float32))
        running = jax.tree.map(jnp.add, running, weight_grads)
        return (running, (result.astype(jnp.bfloat16), input_grads.astype(jnp.bfloat16)))
    zeros = jax.tree.map(jnp.zeros_like, params)
    totals, (outputs, input_grads) = lax.scan(group_step, zeros, (grouped(tokens), grouped(out_grad), grouped(segment_ids), grouped(alive), grouped(masked)))
    masked_total = jnp.sum(masked.astype(jnp.float32))
    factor = N_DP / masked_total
    scaled = tuple((grad * factor for grad in totals))
    correct = (masked > 0) & (predicted == targets)
    row_correct = lax.optimization_barrier(jnp.sum(correct.astype(jnp.int32), axis=1)).astype(jnp.int32)
    counts = jnp.stack([jnp.sum(alive), jnp.sum(masked), jnp.sum(row_correct)]).astype(jnp.int32)
    return (outputs.reshape(tokens.shape), input_grads.reshape(tokens.shape), scaled[0], scaled[1], scaled[2], scaled[3], scaled[4], scaled[5], scaled[6], scaled[7], scaled[8], scaled[9], scaled[10], scaled[11], counts, row_correct)
```

```python
import functools, math
import numpy as np
import jax, jax.numpy as jnp
from jax import lax
from jax.experimental import pallas as pl
from jax.experimental.pallas import tpu as pltpu
from jax.sharding import PartitionSpec as P
BF=jnp.bfloat16; F32=jnp.float32
QB=256; CH=128; TILE=128; HD=32; NEG=-1e9

def nn(a,b): return lax.dot_general(a,b,(((1,),(0,)),((),())),preferred_element_type=F32)
def nt(a,b): return lax.dot_general(a,b,(((1,),(1,)),((),())),preferred_element_type=F32)
def tn(a,b): return lax.dot_general(a,b,(((0,),(0,)),((),())),preferred_element_type=F32)

def seg_start(meta,idx):
    out=jnp.zeros_like(idx)
    for s in range(1,8):
        out=jnp.where(idx>=meta[s],meta[s],out)
    return out

def key_range(meta,first,length,backward):
    live=meta[9]
    lo=jnp.int32(0); hi=jnp.int32(length)
    for s in range(1,8):
        lo=jnp.where(meta[s]<=first,meta[s],lo)
    for s in range(7,0,-1):
        hi=jnp.where(meta[s]>first+QB-1,meta[s],hi)
    if backward:
        hi=jnp.minimum(hi,live)
    else:
        hi=jnp.minimum(hi,jnp.maximum(live,first+QB))
        lo=jnp.where(lo>=live,first,lo)
    k0=lax.div(lo,CH)*CH
    span=jnp.maximum(lax.div(hi+CH-1,CH)*CH-k0,2*CH)
    k0=jnp.minimum(k0,length-span)
    return pl.multiple_of(k0,CH),span

def bias_block(meta,first,k0,w,qn):
    live=meta[9]
    ki=lax.broadcasted_iota(jnp.int32,(w,1),0)+k0
    qi=lax.broadcasted_iota(jnp.int32,(1,qn),1)+first
    ks=jnp.where(ki<live,seg_start(meta,ki),-1)
    qs=seg_start(meta,qi)
    ok=(ks==qs)|(ki==qi)
    return jnp.where(ok,0.0,NEG).astype(F32)

RC=128
def fwd_kernel(meta,q_ref,k_ref,v_ref,o_ref,lse_ref,vt,bias,sbuf,pbuf):
    qb=pl.program_id(1)
    length=k_ref.shape[0]
    first=qb*QB
    @pl.when(qb==0)
    def _():
        vt[...]=v_ref[...].T
    k0,span=key_range(meta,first,length,False)
    lane=lax.broadcasted_iota(jnp.int32,(QB,TILE),1)
    nh=TILE//HD
    for w in range(2*CH,length+1,CH):
        @pl.when(span==w)
        def _(w=w):
            for c in range(0,w,RC):
                bias[c:c+RC,:]=bias_block(meta,first,k0+c,RC,QB)
            q=q_ref[...]
            outs=[]
            def scores(h):
                qm=jnp.where(lax.div(lane,HD)==h,q,jnp.zeros_like(q))
                top=None
                for c in range(0,w,RC):
                    s=nt(k_ref[pl.ds(k0+c,RC),:],qm)+bias[c:c+RC,:]
                    sbuf[h%2,c:c+RC,:]=s
                    t=jnp.max(s.reshape(RC//8,8,QB),axis=0)
                    top=t if top is None else jnp.maximum(top,t)
                return jnp.max(top,axis=0,keepdims=True)
            def rest(h,m):
                tot=None
                for c in range(0,w,RC):
                    e=jnp.exp(sbuf[h%2,c:c+RC,:]-m)
                    t=jnp.sum(e.reshape(RC//8,8,QB),axis=0)
                    tot=t if tot is None else tot+t
                    pbuf[h%2,c:c+RC,:]=e.astype(BF)
                l=jnp.sum(tot,axis=0,keepdims=True)
                o=nn(vt[h*HD:(h+1)*HD,pl.ds(k0,w)],pbuf[h%2,0:w,:])
                outs.append(o/l)
                lse_ref[0,h:h+1,:]=m+jnp.log(l)
            ms=[scores(0)]
            for h in range(nh):
                if h+1<nh: ms.append(scores(h+1))
                rest(h,ms[h])
            o_ref[...]=jnp.concatenate(outs,axis=0).T.astype(BF)

def attend_fwd(meta,q,k,v):
    length,cols=q.shape
    tiles=cols//TILE
    return pl.pallas_call(fwd_kernel,
        out_shape=(jax.ShapeDtypeStruct((length,cols),BF),jax.ShapeDtypeStruct((tiles,TILE//HD,length),F32)),
        grid_spec=pltpu.PrefetchScalarGridSpec(num_scalar_prefetch=1,grid=(tiles,length//QB),
            in_specs=[pl.BlockSpec((QB,TILE),lambda t,b,m:(b,t)),pl.BlockSpec((length,TILE),lambda t,b,m:(0,t)),pl.BlockSpec((length,TILE),lambda t,b,m:(0,t))],
            out_specs=(pl.BlockSpec((QB,TILE),lambda t,b,m:(b,t)),pl.BlockSpec((1,TILE//HD,QB),lambda t,b,m:(t,0,b))),
            scratch_shapes=[pltpu.VMEM((TILE,length),BF),pltpu.VMEM((length,QB),F32),pltpu.VMEM((2,length,QB),F32),pltpu.VMEM((2,length,QB),BF)]),
        compiler_params=pltpu.CompilerParams(vmem_limit_bytes=40<<20),
        cost_estimate=pl.CostEstimate(flops=4*20*32*1024*1024,bytes_accessed=6<<20,transcendentals=0),
        name="attend_fwd")(meta,q,k,v)

def rope_back(x,cos,sin_b):
    y=x*sin_b
    lane=lax.broadcasted_iota(jnp.int32,x.shape,1)
    low=(lane & 16)==0
    return x*cos+jnp.where(low,pltpu.roll(y,TILE-16,1),-pltpu.roll(y,16,1))

def bwd_kernel(meta,q_ref,k_ref,v_ref,o_ref,do_ref,lse_ref,cos_ref,sin_ref,dq_ref,dk_ref,dv_ref,sum_ref,
               kt,bias,pall,dsall,dkacc,dvacc):
    qb=pl.program_id(1); nqb=pl.num_programs(1)
    length=k_ref.shape[0]
    first=pl.multiple_of(qb*QB,QB)
    nh=TILE//HD
    @pl.when(qb==0)
    def _():
        kt[...]=k_ref[...].T
        dkacc[...]=jnp.zeros_like(dkacc)
        dvacc[...]=jnp.zeros_like(dvacc)
        sum_ref[...]=jnp.zeros_like(sum_ref)
        dq_ref[...]=jnp.zeros_like(dq_ref)
    live=meta[9]
    k0,span=key_range(meta,first,length,True)
    lane=lax.broadcasted_iota(jnp.int32,(QB,TILE),1)
    for w in range(2*CH,length+1,CH):
        @pl.when((span==w)&(first<live))
        def _(w=w):
            for c in range(0,w,RC):
                bias[c:c+RC,:]=bias_block(meta,first,k0+c,RC,QB)
            q=q_ref[...]; do=do_ref[...]
            x=do.astype(F32)*o_ref[...].astype(F32)
            hi=x.astype(BF); lo=(x-hi.astype(F32)).astype(BF)
            pick=(lax.div(lax.broadcasted_iota(jnp.int32,(8,TILE),1),HD)==lax.broadcasted_iota(jnp.int32,(8,TILE),0))
            pick=jnp.where(pick,1.0,0.0).astype(BF)
            delta=nt(pick,hi)+nt(pick,lo)
            qms=[];dms=[];dqs=[]
            for h in range(nh):
                mine=lax.div(lane,HD)==h
                qm=jnp.where(mine,q,jnp.zeros_like(q)); dm=jnp.where(mine,do,jnp.zeros_like(do))
                qms.append(qm);dms.append(dm)
                lse_h=lse_ref[0,h:h+1,:]; del_h=delta[h:h+1,:]
                for c in range(0,w,RC):
                    p=jnp.exp(nt(k_ref[pl.ds(k0+c,RC),:],qm)+bias[c:c+RC,:]-lse_h)
                    pall[c:c+RC,h*QB:(h+1)*QB]=p.astype(BF)
                    ds=(p*(nt(v_ref[pl.ds(k0+c,RC),:],dm)-del_h)).astype(BF)
                    dsall[c:c+RC,h*QB:(h+1)*QB]=ds
                dqs.append(nn(kt[h*HD:(h+1)*HD,pl.ds(k0,w)],dsall[0:w,h*QB:(h+1)*QB]))
            dvacc[pl.ds(k0,w),:]+=nn(pall[0:w,:],jnp.concatenate(dms,axis=0))
            dkacc[pl.ds(k0,w),:]+=nn(dsall[0:w,:],jnp.concatenate(qms,axis=0))
            dq=jnp.concatenate(dqs,axis=0).T
            dq=rope_back(dq,cos_ref[pl.ds(first,QB),:],sin_ref[pl.ds(first,QB),:])*(1.0/math.sqrt(HD))
            sum_ref[0,0:1,:]+=jnp.sum(dq,axis=0,keepdims=True)
            dq_ref[pl.ds(first,QB),:]=dq.astype(BF)
    @pl.when(qb==nqb-1)
    def _():
        dk=rope_back(dkacc[...],cos_ref[...],sin_ref[...])
        sum_ref[0,1:2,:]=jnp.sum(dk,axis=0,keepdims=True)
        dk_ref[...]=dk.astype(BF)
        dv=dvacc[...]
        sum_ref[0,2:3,:]=jnp.sum(dv,axis=0,keepdims=True)
        dv_ref[...]=dv.astype(BF)

def attend_bwd(meta,q,k,v,o,do,lse,cos,sin):
    length,cols=q.shape
    tiles=cols//TILE
    blk=pl.BlockSpec((QB,TILE),lambda t,b,m:(b,t)); col=pl.BlockSpec((length,TILE),lambda t,b,m:(0,t)); tab=pl.BlockSpec((length,TILE),lambda t,b,m:(0,0))
    sd=jax.ShapeDtypeStruct
    return pl.pallas_call(bwd_kernel,
        out_shape=(sd((length,cols),BF),)*3+(sd((tiles,8,TILE),F32),),
        grid_spec=pltpu.PrefetchScalarGridSpec(num_scalar_prefetch=1,grid=(tiles,length//QB),
            in_specs=[blk,col,col,blk,blk,pl.BlockSpec((1,TILE//HD,QB),lambda t,b,m:(t,0,b)),tab,tab],
            out_specs=(col,col,col,pl.BlockSpec((1,8,TILE),lambda t,b,m:(t,0,0))),
            scratch_shapes=[pltpu.VMEM((TILE,length),BF),pltpu.VMEM((length,QB),F32),pltpu.VMEM((length,4*QB),BF),pltpu.VMEM((length,4*QB),BF),
                            pltpu.VMEM((length,TILE),F32),pltpu.VMEM((length,TILE),F32)]),
        compiler_params=pltpu.CompilerParams(vmem_limit_bytes=48<<20),
        cost_estimate=pl.CostEstimate(flops=10*20*32*1024*1024,bytes_accessed=10<<20,transcendentals=0),
        name="attend_bwd")(meta,q,k,v,o,do,lse,cos,sin)
EPS=1e-5
TB=256
def ln_stats(x):
    mu=jnp.mean(x,axis=-1,keepdims=True)
    c=x-mu
    var=jnp.mean(c*c,axis=-1,keepdims=True)
    r=lax.rsqrt(var+EPS)
    return c*r,r

def rope_tables(length):
    lane=np.arange(TILE)%(HD//2)
    inv=np.exp(lane.astype(np.float64)*(-2.0*math.log(10000.0)/HD))
    ang=np.arange(length,dtype=np.float64)[:,None]*inv[None,:]
    return np.cos(ang).astype(np.float32),np.sin(ang).astype(np.float32)

def qkv_kernel(meta,x_ref,wo_ref,wp_ref,b_ref,g_ref,s_ref,ct_ref,st_ref,n_ref,q_ref,k_ref,v_ref,cos_ref,sin_ref,wc_ref):
    i=pl.program_id(0)
    half=wo_ref.shape[2]
    @pl.when(i==0)
    def _():
        for c in range(3):
            wc_ref[c]=jnp.concatenate([wo_ref[c],wp_ref[c]],axis=1)
    x=x_ref[...].astype(F32)
    nrm,_=ln_stats(x)
    n=(nrm*g_ref[...].astype(F32)+s_ref[...].astype(F32)).astype(BF)
    n_ref[...]=n
    first=i*TB
    top=ct_ref.shape[0]-1
    j=lax.broadcasted_iota(jnp.int32,(TB,TILE),0)+first
    cc=jnp.broadcast_to(ct_ref[0:1,:],(TB,TILE)); ss=jnp.broadcast_to(st_ref[0:1,:],(TB,TILE))
    for s in range(1,8):
        at=meta[s]; row=jnp.minimum(at,top)
        past=j>=at
        cc=jnp.where(past,ct_ref[pl.ds(row,1),:],cc)
        ss=jnp.where(past,st_ref[pl.ds(row,1),:],ss)
    cj=ct_ref[pl.ds(pl.multiple_of(first,TB),TB),:]; sj=st_ref[pl.ds(pl.multiple_of(first,TB),TB),:]
    cos=cj*cc+sj*ss; sin=sj*cc-cj*ss
    cos_ref[...]=cos; sin_ref[...]=sin
    low=(lax.broadcasted_iota(jnp.int32,(TB,TILE),1)&16)==0
    signed=jnp.where(low,-sin,sin)
    for c,(out,scale) in enumerate(((q_ref,1.0/math.sqrt(HD)),(k_ref,None),(v_ref,None))):
        p=nn(n,wc_ref[c])+b_ref[c:c+1,:]
        if c==2:
            out[...]=p.astype(BF)
        else:
            for t in range(p.shape[1]//TILE):
                y=p[:,t*TILE:(t+1)*TILE]
                z=y*cos+jnp.where(low,pltpu.roll(y,TILE-16,1),pltpu.roll(y,16,1))*signed
                if scale is not None: z=z*scale
                out[:,t*TILE:(t+1)*TILE]=z.astype(BF)

def full(shape):
    return pl.BlockSpec(shape,lambda *a:(0,)*len(shape))
def params(mb): return pltpu.CompilerParams(vmem_limit_bytes=mb<<20)
sd=jax.ShapeDtypeStruct

def qkv_call(meta,x,w_own,w_par,b,g,s):
    T,D=x.shape; half=w_own.shape[2]; inner=2*half
    ct,st=rope_tables(T)
    rows=lambda n:pl.BlockSpec((TB,n),lambda i,m:(i,0))
    return pl.pallas_call(qkv_kernel,
        out_shape=(sd((T,D),BF),sd((T,inner),BF),sd((T,inner),BF),sd((T,inner),BF),sd((T,TILE),F32),sd((T,TILE),F32),sd((3,D,inner),BF)),
        grid_spec=pltpu.PrefetchScalarGridSpec(num_scalar_prefetch=1,grid=(T//TB,),
            in_specs=[rows(D),full(w_own.shape),full(w_par.shape),full((3,inner)),full((1,D)),full((1,D)),full((T,TILE)),full((T,TILE))],
            out_specs=(rows(D),rows(inner),rows(inner),rows(inner),rows(TILE),rows(TILE),full((3,D,inner)))),
        compiler_params=params(44),
        cost_estimate=pl.CostEstimate(flops=2*T*D*3*inner,bytes_accessed=12<<20,transcendentals=0),
        name="norm_qkv_rope")(meta,x,w_own,w_par,b,g,s,jnp.asarray(ct),jnp.asarray(st))

def gelu_parts(h):
    cdf=0.5*(1.0+lax.erf(h*(1.0/math.sqrt(2.0))))
    return h*cdf, cdf+h*jnp.exp(-0.5*h*h)*(1.0/math.sqrt(2.0*math.pi))

FC=256
def ffn_kernel(meta,mix_ref,x_ref,og_ref,tg_ref,woo_ref,wop_ref,bo_ref,g_ref,s_ref,wuo_ref,wup_ref,buo_ref,bup_ref,wdo_ref,wdp_ref,bd_ref,
               n2_ref,dl_ref,ao_ref,ap_ref,uo_ref,up_ref,out_ref,mg_ref,bl_ref,xg_ref,sum_ref,sbo_ref,sbp_ref,wo,feed,sg):
    i=pl.program_id(0)
    @pl.when(i==0)
    def _():
        wo[...]=jnp.concatenate([woo_ref[...],wop_ref[...]],axis=0)
        sum_ref[...]=jnp.zeros_like(sum_ref); sbo_ref[...]=jnp.zeros_like(sbo_ref); sbp_ref[...]=jnp.zeros_like(sbp_ref)
    live=meta[9]
    mid=x_ref[...].astype(F32)+nn(mix_ref[...],wo[...])+bo_ref[...].astype(F32)
    nrm,r=ln_stats(mid)
    g=g_ref[...].astype(F32)
    n2=(nrm*g+s_ref[...].astype(F32)).astype(BF)
    n2_ref[...]=n2
    at=lax.broadcasted_iota(jnp.int32,(8,TB),1)+i*TB
    keep=jnp.where((tg_ref[...]>=0)&(at<live),1.0,0.0)
    keep=keep.T[:,0:1]
    top=og_ref[...].astype(F32)*keep
    dl=top.astype(BF)
    dl_ref[...]=dl
    sum_ref[3:4,:]+=jnp.sum(top,axis=0,keepdims=True)
    first=True
    for wu,bu,wd,a_ref,u_ref,sb in ((wuo_ref,buo_ref,wdo_ref,ao_ref,uo_ref,sbo_ref),(wup_ref,bup_ref,wdp_ref,ap_ref,up_ref,sbp_ref)):
        for c in range(0,wu.shape[1],FC):
            h=nn(n2,wu[:,c:c+FC])+bu[:,c:c+FC].astype(F32)
            ag=nt(dl,wd[c:c+FC,:])
            val,slope=gelu_parts(h)
            a=val.astype(BF)
            hg=ag*slope
            u=hg.astype(BF)
            a_ref[:,c:c+FC]=a; u_ref[:,c:c+FC]=u
            sb[0:1,c:c+FC]+=jnp.sum(hg,axis=0,keepdims=True)
    feed=nn(ao_ref[...],wdo_ref[...])+nn(ap_ref[...],wdp_ref[...])
    out_ref[...]=(mid+feed+bd_ref[...].astype(F32)).astype(BF)
    sg=nt(uo_ref[...],wuo_ref[...])+nt(up_ref[...],wup_ref[...])
    sum_ref[0:1,:]+=jnp.sum(sg*nrm,axis=0,keepdims=True)
    sum_ref[1:2,:]+=jnp.sum(sg,axis=0,keepdims=True)
    inner=sg*g
    mg=top+r*(inner-jnp.mean(inner,axis=-1,keepdims=True)-nrm*jnp.mean(inner*nrm,axis=-1,keepdims=True))
    mg_ref[...]=mg
    sum_ref[2:3,:]+=jnp.sum(mg,axis=0,keepdims=True)
    bl=mg.astype(BF)
    bl_ref[...]=bl
    xg_ref[...]=nt(bl,wo[...]).astype(BF)

def ffn_call(meta,mixed,x,og,targets,wo_own,wo_par,b_out,g,s,wu_own,wu_par,bu_own,bu_par,wd_own,wd_par,b_down):
    T,D=x.shape; inner=mixed.shape[1]; fh=wu_own.shape[1]
    rows=lambda n:pl.BlockSpec((TB,n),lambda i,m:(i,0))
    one=full((1,D))
    return pl.pallas_call(ffn_kernel,
        out_shape=(sd((T,D),BF),sd((T,D),BF),sd((T,fh),BF),sd((T,fh),BF),sd((T,fh),BF),sd((T,fh),BF),sd((T,D),BF),sd((T,D),F32),sd((T,D),BF),sd((T,inner),BF),
                   sd((8,D),F32),sd((8,fh),F32),sd((8,fh),F32)),
        grid_spec=pltpu.PrefetchScalarGridSpec(num_scalar_prefetch=1,grid=(T//TB,),
            in_specs=[rows(inner),rows(D),rows(D),pl.BlockSpec((1,TB),lambda i,m:(0,i)),full(wo_own.shape),full(wo_par.shape),one,one,one,
                      full(wu_own.shape),full(wu_par.shape),full((1,fh)),full((1,fh)),full(wd_own.shape),full(wd_par.shape),one],
            out_specs=(rows(D),rows(D),rows(fh),rows(fh),rows(fh),rows(fh),rows(D),rows(D),rows(D),rows(inner),full((8,D)),full((8,fh)),full((8,fh))),
            scratch_shapes=[pltpu.VMEM((inner,D),BF),pltpu.VMEM((TB,D),F32),pltpu.VMEM((TB,D),F32)]),
        compiler_params=params(56),
        cost_estimate=pl.CostEstimate(flops=2*T*D*(2*inner+8*fh),bytes_accessed=30<<20,transcendentals=0),
        name="mix_ffn_both_ways")(meta,mixed,x,og,targets,wo_own,wo_par,b_out,g,s,wu_own,wu_par,bu_own,bu_par,wd_own,wd_par,b_down)

def ffn_grads_kernel(n_ref,dl_ref,mix_ref,bl_ref,ao_ref,ap_ref,uo_ref,up_ref,guo_ref,gup_ref,gdo_ref,gdp_ref,goo_ref,gop_ref,nT):
    i=pl.program_id(0)
    @pl.when(i==0)
    def _():
        nT[...]=n_ref[...].T
        go=tn(mix_ref[...],bl_ref[...]).astype(BF)
        h=goo_ref.shape[0]
        goo_ref[...]=go[0:h]; gop_ref[...]=go[h:2*h]
    guo_ref[...]=nn(nT[...],uo_ref[...]).astype(BF)
    gup_ref[...]=nn(nT[...],up_ref[...]).astype(BF)
    gdo_ref[...]=tn(ao_ref[...],dl_ref[...]).astype(BF)
    gdp_ref[...]=tn(ap_ref[...],dl_ref[...]).astype(BF)

def ffn_grads_call(n2,dl,mixed,bl,ao,ap,uo,up):
    T,D=n2.shape; fh=ao.shape[1]; inner=mixed.shape[1]
    cols=pl.BlockSpec((T,FC),lambda i:(0,i))
    wide=pl.BlockSpec((D,FC),lambda i:(0,i)); tall=pl.BlockSpec((FC,D),lambda i:(i,0))
    return pl.pallas_call(ffn_grads_kernel,
        out_shape=(sd((D,fh),BF),sd((D,fh),BF),sd((fh,D),BF),sd((fh,D),BF),sd((inner//2,D),BF),sd((inner//2,D),BF)),
        grid=(fh//FC,),
        in_specs=[full((T,D)),full((T,D)),full((T,inner)),full((T,D)),cols,cols,cols,cols],
        out_specs=(wide,wide,tall,tall,full((inner//2,D)),full((inner//2,D))),
        scratch_shapes=[pltpu.VMEM((D,T),BF)],
        compiler_params=params(48),
        cost_estimate=pl.CostEstimate(flops=2*T*D*(4*fh+inner),bytes_accessed=24<<20,transcendentals=0),
        name="ffn_weight_grads")(n2,dl,mixed,bl,ao,ap,uo,up)

def in_grad_kernel(dq_ref,dk_ref,dv_ref,w_ref,x_ref,mg_ref,g_ref,out_ref,sum_ref):
    i=pl.program_id(0)
    @pl.when(i==0)
    def _():
        sum_ref[...]=jnp.zeros_like(sum_ref)
    fg=nt(dq_ref[...],w_ref[0])+nt(dk_ref[...],w_ref[1])+nt(dv_ref[...],w_ref[2])
    nrm,r=ln_stats(x_ref[...].astype(F32))
    sum_ref[0:1,:]+=jnp.sum(fg*nrm,axis=0,keepdims=True)
    sum_ref[1:2,:]+=jnp.sum(fg,axis=0,keepdims=True)
    inner=fg*g_ref[...].astype(F32)
    out_ref[...]=(mg_ref[...]+r*(inner-jnp.mean(inner,axis=-1,keepdims=True)-nrm*jnp.mean(inner*nrm,axis=-1,keepdims=True))).astype(BF)

def in_grad_call(dq,dk,dv,wc,x,mg,g):
    T,D=x.shape; inner=dq.shape[1]
    rows=lambda n:pl.BlockSpec((TB,n),lambda i:(i,0))
    return pl.pallas_call(in_grad_kernel,
        out_shape=(sd((T,D),BF),sd((8,D),F32)),grid=(T//TB,),
        in_specs=[rows(inner)]*3+[full(wc.shape),rows(D),rows(D),full((1,D))],
        out_specs=(rows(D),full((8,D))),
        compiler_params=params(40),
        cost_estimate=pl.CostEstimate(flops=6*T*D*inner,bytes_accessed=14<<20,transcendentals=0),
        name="input_grad")(dq,dk,dv,wc,x,mg,g)

def qkv_grads_kernel(n_ref,dq_ref,dk_ref,dv_ref,own_ref,par_ref):
    nT=n_ref[...].T
    half=own_ref.shape[2]
    for c,r in enumerate((dq_ref,dk_ref,dv_ref)):
        g=nn(nT,r[...]).astype(BF)
        own_ref[c]=g[:,0:half]; par_ref[c]=g[:,half:2*half]

def qkv_grads_call(n1,dq,dk,dv):
    T,D=n1.shape; inner=dq.shape[1]
    return pl.pallas_call(qkv_grads_kernel,
        out_shape=(sd((3,D,inner//2),BF),)*2,
        compiler_params=params(48),
        in_specs=[pl.BlockSpec(memory_space=pltpu.VMEM)]*4,out_specs=(pl.BlockSpec(memory_space=pltpu.VMEM),)*2,
        cost_estimate=pl.CostEstimate(flops=6*T*D*inner,bytes_accessed=8<<20,transcendentals=0),
        name="qkv_weight_grads")(n1,dq,dk,dv)


def swap_cores(a):
    return lax.ppermute(a,"tensor",[(0,1),(1,0)])

def sum_everywhere(a):
    n=lax.axis_size("dp")
    a=a+swap_cores(a)
    step=1
    while step<n:
        a=a+lax.ppermute(a,"dp",[(i,i^step) for i in range(n)])
        step*=2
    return a

def body(tokens,out_grad,segment_ids,token_live,live_rows,targets,predicted,w_qkv,b_qkv,w_out,b_out,
         norm1_gain,norm1_bias,norm2_gain,norm2_bias,w_up,b_up,w_down,b_down):
    member=lax.axis_index("tensor")
    x=tokens[0]; T,D=x.shape
    half=w_qkv.shape[2]; fh=w_up.shape[1]
    w_qkv_p=swap_cores(w_qkv)
    bias_own=jnp.concatenate([b_qkv.reshape(1,3*half),b_up.reshape(1,fh)],axis=1)
    bias_par=swap_cores(bias_own)
    w_out_p=swap_cores(w_out); w_up_p=swap_cores(w_up); w_down_p=swap_cores(w_down)
    segments=lax.dynamic_index_in_dim(segment_ids,member,0,keepdims=False)
    lived=lax.dynamic_index_in_dim(token_live,member,0,keepdims=False)
    starts=jnp.sum((segments[None,:]<jnp.arange(9,dtype=jnp.int32)[:,None]).astype(jnp.int32),axis=1)
    live=jnp.where(member<live_rows[0],jnp.sum(lived),0)
    meta=jnp.concatenate([starts,live[None],jnp.zeros((6,),jnp.int32)])
    row=lambda a:a.reshape(1,-1)
    b_cat=jnp.concatenate([bias_own[:,:3*half].reshape(3,half),bias_par[:,:3*half].reshape(3,half)],axis=1).astype(F32)
    g1,s1,g2,s2=row(norm1_gain),row(norm1_bias),row(norm2_gain),row(norm2_bias)
    n1,q,k,v,cos,sin,wc=qkv_call(meta,x,w_qkv,w_qkv_p,b_cat,g1,s1)
    mixed,lse=attend_fwd(meta,q,k,v)
    n2,dl,ao,ap,uo,up,out_act,mg,bl,xg,sums,sbo,sbp=ffn_call(meta,mixed,x,out_grad[0],targets,w_out,w_out_p,row(b_out),g2,s2,
        w_up,w_up_p,bias_own[:,3*half:],bias_par[:,3*half:],w_down,w_down_p,row(b_down))
    guo,gup,gdo,gdp,goo,gop=ffn_grads_call(n2,dl,mixed,bl,ao,ap,uo,up)
    join=lambda o,p:(o.astype(F32)+swap_cores(p).astype(F32)).astype(BF)
    ffn=lax.psum((join(guo,gup),join(gdo,gdp),join(goo,gop)),"dp")
    dq,dk,dv,psum3=attend_bwd(meta,q,k,v,mixed,xg,lse,cos,sin)
    in_grad,sums1=in_grad_call(dq,dk,dv,wc,x,mg,g1)
    gqo,gqp=qkv_grads_call(n1,dq,dk,dv)
    gqkv=lax.psum(join(gqo,gqp),"dp")
    masked=(targets[0]>=0)&(jnp.arange(T)<live)
    correct=masked&(predicted[0]==targets[0])
    row_correct=jnp.sum(correct.astype(jnp.int32))[None]
    tallies=jnp.stack([live.astype(F32),jnp.sum(masked.astype(F32)),row_correct[0].astype(F32)])
    bq=psum3[:,0:3,:].transpose(1,0,2).reshape(3,2*half)
    own=jnp.concatenate([bq[:,:half].reshape(-1),sbo[0]]); par=jnp.concatenate([bq[:,half:].reshape(-1),sbp[0]])
    shared=jnp.concatenate([sums[2],sums[3],sums1[0],sums1[1],sums[0],sums[1],tallies,jnp.zeros((-(3*half+fh+6*D+3)%TILE,),F32)])
    small=jnp.concatenate([own,shared]).reshape(-1,TILE)
    other=jnp.concatenate([par,shared]).reshape(-1,TILE)
    small=small+swap_cores(other)
    n=lax.axis_size("dp"); step=1
    while step<n:
        small=small+lax.ppermute(small,"dp",[(i,i^step) for i in range(n)])
        step*=2
    small=small.reshape(-1)
    base=3*half+fh
    totals=small[base+6*D:base+6*D+3]
    factor=n/totals[1]
    part=lambda i:small[base+i*D:base+(i+1)*D]*factor
    return (out_act[None],in_grad[None],gqkv.astype(F32)*factor,small[:3*half].reshape(3,half)*factor,ffn[2].astype(F32)*factor,part(0),
            part(2),part(3),part(4),part(5),ffn[0].astype(F32)*factor,small[3*half:base]*factor,ffn[1].astype(F32)*factor,part(1),
            totals.astype(jnp.int32),row_correct)


def solution(mesh):
    in_specs = (
        P(("dp", "tensor"), None, None),
        P(("dp", "tensor"), None, None),
        P("dp", None),
        P("dp", None),
        P("dp"),
        P(("dp", "tensor"), None),
        P(("dp", "tensor"), None),
        P(None, None, "tensor"),
        P(None, "tensor"),
        P("tensor", None),
        P(),
        P(),
        P(),
        P(),
        P(),
        P(None, "tensor"),
        P("tensor"),
        P("tensor", None),
        P(),
    )
    out_specs = (
        P(("dp", "tensor"), None, None),
        P(("dp", "tensor"), None, None),
        P(None, None, "tensor"),
        P(None, "tensor"),
        P("tensor", None),
        P(),
        P(),
        P(),
        P(),
        P(),
        P(None, "tensor"),
        P("tensor"),
        P("tensor", None),
        P(),
        P(),
        P(("dp", "tensor")),
    )
    return jax.shard_map(body, mesh=mesh, in_specs=in_specs, out_specs=out_specs, check_vma=False)
```

```python
import functools, math
import numpy as np
import jax, jax.numpy as jnp
from jax import lax
from jax.experimental import pallas as pl
from jax.experimental.pallas import tpu as pltpu
from jax.sharding import PartitionSpec as P
BF=jnp.bfloat16; F32=jnp.float32
QB=256; CH=128; TILE=128; HD=32; NEG=-1e9

def nn(a,b): return lax.dot_general(a,b,(((1,),(0,)),((),())),preferred_element_type=F32)
def nt(a,b): return lax.dot_general(a,b,(((1,),(1,)),((),())),preferred_element_type=F32)
def tn(a,b): return lax.dot_general(a,b,(((0,),(0,)),((),())),preferred_element_type=F32)

def seg_start(meta,idx):
    out=jnp.zeros_like(idx)
    for s in range(1,8):
        out=jnp.where(idx>=meta[s],meta[s],out)
    return out

def key_range(meta,first,length,backward):
    live=meta[9]
    lo=jnp.int32(0); hi=jnp.int32(length)
    for s in range(1,8):
        lo=jnp.where(meta[s]<=first,meta[s],lo)
    for s in range(7,0,-1):
        hi=jnp.where(meta[s]>first+QB-1,meta[s],hi)
    if backward:
        hi=jnp.minimum(hi,live)
    else:
        hi=jnp.minimum(hi,jnp.maximum(live,first+QB))
        lo=jnp.where(lo>=live,first,lo)
    k0=lax.div(lo,CH)*CH
    span=jnp.maximum(lax.div(hi+CH-1,CH)*CH-k0,2*CH)
    k0=jnp.minimum(k0,length-span)
    return pl.multiple_of(k0,CH),span

def query_span(meta,first,qn):
    live=meta[9]
    qi=lax.broadcasted_iota(jnp.int32,(8,qn),1)+first
    lo=jnp.zeros_like(qi); hi=jnp.full_like(qi,meta[8])
    for s in range(1,8):
        lo=jnp.where(qi>=meta[s],meta[s],lo)
    for s in range(7,0,-1):
        hi=jnp.where(qi<meta[s],meta[s],hi)
    return qi,lo,jnp.minimum(hi,live)

def bias_rows(spans,k0,rows,diagonal):
    qi,lo,hi=spans
    ki=lax.broadcasted_iota(jnp.int32,qi.shape,0)+k0
    out=[]
    for r in range(0,rows,8):
        at=ki+r
        ok=(at>=lo)&(at<hi)
        if diagonal: ok=ok|(at==qi)
        out.append(jnp.where(ok,0.0,NEG))
    return jnp.concatenate(out,axis=0)

RCX=256
PAIR=1
def chunks(w):
    return [(c,min(RCX,w-c)) for c in range(0,w,RCX)]
def fwd_kernel(meta,q_ref,k_ref,v_ref,o_ref,lse_ref,vt,bias,sbuf,pbuf):
    length=k_ref.shape[0]
    vt[...]=v_ref[...].T
    lane=lax.broadcasted_iota(jnp.int32,(QB,TILE),1)
    lax.fori_loop(0,length//QB,lambda qb,_:fwd_block(qb,meta,q_ref,k_ref,o_ref,lse_ref,vt,bias,sbuf,pbuf,lane,length),0)

def fwd_block(qb,meta,q_ref,k_ref,o_ref,lse_ref,vt,bias,sbuf,pbuf,lane,length):
    first=pl.multiple_of(qb*QB,QB)
    k0,span=key_range(meta,first,length,False)
    nh=TILE//HD
    for w in range(2*CH,length+1,CH):
        @pl.when(span==w)
        def _(w=w):
            spans=query_span(meta,first,QB)
            for c,RC in chunks(w):
                bias[c:c+RC,:]=bias_rows(spans,k0+c,RC,True)
            q=q_ref[pl.ds(first,QB),:]
            outs=[]
            def scores(h):
                qm=jnp.where(lax.div(lane,HD)==h,q,jnp.zeros_like(q))
                top=None
                for c,RC in chunks(w):
                    s=nt(k_ref[pl.ds(k0+c,RC),:],qm)+bias[c:c+RC,:]
                    sbuf[h%2,c:c+RC,:]=s
                    t=jnp.max(s.reshape(RC//8,8,QB),axis=0)
                    top=t if top is None else jnp.maximum(top,t)
                return jnp.max(top,axis=0,keepdims=True)
            def rest(h,m):
                tot=None
                for c,RC in chunks(w):
                    e=jnp.exp(sbuf[h%2,c:c+RC,:]-m)
                    t=jnp.sum(e.reshape(RC//8,8,QB),axis=0)
                    tot=t if tot is None else tot+t
                    pbuf[h%2,c:c+RC,:]=e.astype(BF)
                l=jnp.sum(tot,axis=0,keepdims=True)
                o=nn(vt[h*HD:(h+1)*HD,pl.ds(k0,w)],pbuf[h%2,0:w,:])
                outs.append(o/l)
                lse_ref[0,h:h+1,pl.ds(first,QB)]=m+jnp.log(l)
            ms=[scores(0)]
            for h in range(nh):
                if h+1<nh: ms.append(scores(h+1))
                rest(h,ms[h])
            o_ref[pl.ds(first,QB),:]=jnp.concatenate(outs,axis=0).T.astype(BF)
    return 0

def attend_fwd(meta,q,k,v):
    length,cols=q.shape
    tiles=cols//TILE
    return pl.pallas_call(fwd_kernel,
        out_shape=(jax.ShapeDtypeStruct((length,cols),BF),jax.ShapeDtypeStruct((tiles,TILE//HD,length),F32)),
        grid_spec=pltpu.PrefetchScalarGridSpec(num_scalar_prefetch=1,grid=(tiles,),
            in_specs=[pl.BlockSpec((length,TILE),lambda t,m:(0,t))]*3,
            out_specs=(pl.BlockSpec((length,TILE),lambda t,m:(0,t)),pl.BlockSpec((1,TILE//HD,length),lambda t,m:(t,0,0))),
            scratch_shapes=[pltpu.VMEM((TILE,length),BF),pltpu.VMEM((length,QB),F32),pltpu.VMEM((2,length,QB),F32),pltpu.VMEM((2,length,QB),BF)]),
        compiler_params=pltpu.CompilerParams(vmem_limit_bytes=40<<20),
        cost_estimate=pl.CostEstimate(flops=4*20*32*1024*1024,bytes_accessed=6<<20,transcendentals=0),
        name="attend_fwd")(meta,q,k,v)

def rope_back(x,cos,sin_b):
    y=x*sin_b
    lane=lax.broadcasted_iota(jnp.int32,x.shape,1)
    low=(lane & 16)==0
    return x*cos+jnp.where(low,pltpu.roll(y,TILE-16,1),-pltpu.roll(y,16,1))

def bwd_kernel(nin,meta,q_ref,k_ref,v_ref,o_ref,do_ref,lse_ref,cos_ref,sin_ref,*rest):
    dq_ref,dk_ref,dv_ref,sum_ref,kt,bias,pall,dsall,dkacc,dvacc=rest[nin:]
    length=k_ref.shape[0]
    kt[...]=k_ref[...].T
    dkacc[...]=jnp.zeros_like(dkacc)
    dvacc[...]=jnp.zeros_like(dvacc)
    sum_ref[...]=jnp.zeros_like(sum_ref)
    lane=lax.broadcasted_iota(jnp.int32,(QB,TILE),1)
    def block(qb,_):
        bwd_block(qb,meta,q_ref,k_ref,v_ref,o_ref,do_ref,lse_ref,cos_ref,sin_ref,dq_ref,sum_ref,kt,bias,pall,dsall,dkacc,dvacc,lane,length)
        return 0
    lax.fori_loop(0,length//QB,block,0)
    dk=rope_back(dkacc[...],cos_ref[...],sin_ref[...])
    sum_ref[0,1:2,:]=jnp.sum(dk,axis=0,keepdims=True)
    dk_ref[...]=dk.astype(BF)
    dv=dvacc[...]
    sum_ref[0,2:3,:]=jnp.sum(dv,axis=0,keepdims=True)
    dv_ref[...]=dv.astype(BF)

def bwd_block(qb,meta,q_ref,k_ref,v_ref,o_ref,do_ref,lse_ref,cos_ref,sin_ref,dq_ref,sum_ref,kt,bias,pall,dsall,dkacc,dvacc,lane,length):
    first=pl.multiple_of(qb*QB,QB)
    nh=TILE//HD
    live=meta[9]
    k0,span=key_range(meta,first,length,True)
    @pl.when(first>=live)
    def _():
        dq_ref[pl.ds(first,QB),:]=jnp.zeros((QB,TILE),BF)
    for w in range(2*CH,length+1,CH):
        @pl.when((span==w)&(first<live))
        def _(w=w):
            spans=query_span(meta,first,QB)
            for c,RC in chunks(w):
                bias[c:c+RC,:]=bias_rows(spans,k0+c,RC,False)
            q=q_ref[pl.ds(first,QB),:]; do=do_ref[pl.ds(first,QB),:]
            x=do.astype(F32)*o_ref[pl.ds(first,QB),:].astype(F32)
            hi=x.astype(BF); lo=(x-hi.astype(F32)).astype(BF)
            pick=(lax.div(lax.broadcasted_iota(jnp.int32,(8,TILE),1),HD)==lax.broadcasted_iota(jnp.int32,(8,TILE),0))
            pick=jnp.where(pick,1.0,0.0).astype(BF)
            delta=nt(pick,hi)+nt(pick,lo)
            qms=[];dms=[];dqs=[]
            def scores(h):
                mine=lax.div(lane,HD)==h
                qm=jnp.where(mine,q,jnp.zeros_like(q)); dm=jnp.where(mine,do,jnp.zeros_like(do))
                qms.append(qm);dms.append(dm)
                lse_h=lse_ref[0,h:h+1,pl.ds(first,QB)]; del_h=delta[h:h+1,:]
                for c,RC in chunks(w):
                    p=jnp.exp(nt(k_ref[pl.ds(k0+c,RC),:],qm)+bias[c:c+RC,:]-lse_h)
                    pall[c:c+RC,h*QB:(h+1)*QB]=p.astype(BF)
                    ds=(p*(nt(v_ref[pl.ds(k0+c,RC),:],dm)-del_h)).astype(BF)
                    dsall[c:c+RC,h*QB:(h+1)*QB]=ds
            def grads(h):
                dqs.append(nn(kt[h*HD:(h+1)*HD,pl.ds(k0,w)],dsall[0:w,h*QB:(h+1)*QB]))
                if h%PAIR==PAIR-1:
                    lo=h+1-PAIR
                    for c,RC in chunks(w):
                        at=pl.ds(k0+c,RC)
                        dvacc[at,:]+=nn(pall[c:c+RC,lo*QB:(h+1)*QB],jnp.concatenate(dms[lo:h+1],axis=0))
                        dkacc[at,:]+=nn(dsall[c:c+RC,lo*QB:(h+1)*QB],jnp.concatenate(qms[lo:h+1],axis=0))
            for h in range(nh):
                scores(h)
                if h: grads(h-1)
            grads(nh-1)
            dq=jnp.concatenate(dqs,axis=0).T
            dq=rope_back(dq,cos_ref[pl.ds(first,QB),:],sin_ref[pl.ds(first,QB),:])*(1.0/math.sqrt(HD))
            sum_ref[0,0:1,:]+=jnp.sum(dq,axis=0,keepdims=True)
            dq_ref[pl.ds(first,QB),:]=dq.astype(BF)

def attend_bwd(meta,q,k,v,o,do,lse,cos,sin,begin,count,held):
    length,cols=q.shape
    tiles=cols//TILE
    col=pl.BlockSpec((length,TILE),lambda t,m:(0,begin+t)); tab=pl.BlockSpec((length,TILE),lambda t,m:(0,0))
    sd=jax.ShapeDtypeStruct
    held=() if held is None else tuple(held)
    return pl.pallas_call(functools.partial(bwd_kernel,len(held)),
        out_shape=(sd((length,cols),BF),)*3+(sd((tiles,8,TILE),F32),),
        grid_spec=pltpu.PrefetchScalarGridSpec(num_scalar_prefetch=1,grid=(count,),
            in_specs=[col]*5+[pl.BlockSpec((1,TILE//HD,length),lambda t,m:(begin+t,0,0)),tab,tab]+[pl.BlockSpec(memory_space=pl.ANY)]*len(held),
            out_specs=(col,col,col,pl.BlockSpec((1,8,TILE),lambda t,m:(begin+t,0,0))),
            scratch_shapes=[pltpu.VMEM((TILE,length),BF),pltpu.VMEM((length,QB),F32),pltpu.VMEM((length,4*QB),BF),pltpu.VMEM((length,4*QB),BF),
                            pltpu.VMEM((length,TILE),F32),pltpu.VMEM((length,TILE),F32)]),
        input_output_aliases={9+i:i for i in range(len(held))},
        compiler_params=pltpu.CompilerParams(vmem_limit_bytes=48<<20),
        cost_estimate=pl.CostEstimate(flops=count*4*32*16*1024*1024,bytes_accessed=count*(2<<20),transcendentals=0),
        name="attend_bwd")(meta,q,k,v,o,do,lse,cos,sin,*held)
EPS=1e-5
TB=256
HALF=TILE//2
def weave(out,own,par):
    for t in range(own.shape[0]//HALF):
        out[t*TILE:t*TILE+HALF,:]=own[t*HALF:(t+1)*HALF,:]
        out[t*TILE+HALF:(t+1)*TILE,:]=par[t*HALF:(t+1)*HALF,:]

def unweave(a):
    n=a.shape[0]//TILE
    return (jnp.concatenate([a[t*TILE:t*TILE+HALF] for t in range(n)],axis=0),
            jnp.concatenate([a[t*TILE+HALF:(t+1)*TILE] for t in range(n)],axis=0))

def ln_stats(x):
    mu=jnp.mean(x,axis=-1,keepdims=True)
    c=x-mu
    var=jnp.mean(c*c,axis=-1,keepdims=True)
    r=lax.rsqrt(var+EPS)
    return c*r,r

def rope_tables(length):
    lane=np.arange(TILE)%(HD//2)
    inv=np.exp(lane.astype(np.float64)*(-2.0*math.log(10000.0)/HD))
    ang=np.arange(length,dtype=np.float64)[:,None]*inv[None,:]
    return np.cos(ang).astype(np.float32),np.sin(ang).astype(np.float32)

def qkv_kernel(meta,x_ref,wo_ref,wp_ref,bo_ref,bp_ref,vec_ref,ct_ref,st_ref,n_ref,q_ref,k_ref,v_ref,cos_ref,sin_ref,wc_ref,b_ref):
    i=pl.program_id(0)
    @pl.when(i==0)
    def _():
        for c in range(3):
            weave(wc_ref.at[c],wo_ref.at[c],wp_ref.at[c])
            at=bo_ref.shape[1]-3*wo_ref.shape[1]+c*wo_ref.shape[1]
            b_ref[c:c+1,:]=jnp.concatenate([r[0:1,at+t*HALF:at+(t+1)*HALF] for t in range(wo_ref.shape[1]//HALF) for r in (bo_ref,bp_ref)],axis=1)
    x=x_ref[...].astype(F32)
    nrm,_=ln_stats(x)
    n=(nrm*vec_ref[0:1,:]+vec_ref[1:2,:]).astype(BF)
    n_ref[...]=n
    first=i*TB
    top=ct_ref.shape[0]-1
    j=lax.broadcasted_iota(jnp.int32,(TB,TILE),0)+first
    cc=jnp.broadcast_to(ct_ref[0:1,:],(TB,TILE)); ss=jnp.broadcast_to(st_ref[0:1,:],(TB,TILE))
    for s in range(1,8):
        at=meta[s]; row=jnp.minimum(at,top)
        past=j>=at
        cc=jnp.where(past,ct_ref[pl.ds(row,1),:],cc)
        ss=jnp.where(past,st_ref[pl.ds(row,1),:],ss)
    cj=ct_ref[pl.ds(pl.multiple_of(first,TB),TB),:]; sj=st_ref[pl.ds(pl.multiple_of(first,TB),TB),:]
    cos=cj*cc+sj*ss; sin=sj*cc-cj*ss
    cos_ref[...]=cos; sin_ref[...]=sin
    low=(lax.broadcasted_iota(jnp.int32,(TB,TILE),1)&16)==0
    signed=jnp.where(low,-sin,sin)
    for c,(out,scale) in enumerate(((q_ref,1.0/math.sqrt(HD)),(k_ref,None),(v_ref,None))):
        p=nt(n,wc_ref[c])+b_ref[c:c+1,:]
        if c==2:
            out[...]=p.astype(BF)
        else:
            for t in range(p.shape[1]//TILE):
                y=p[:,t*TILE:(t+1)*TILE]
                z=y*cos+jnp.where(low,pltpu.roll(y,TILE-16,1),pltpu.roll(y,16,1))*signed
                if scale is not None: z=z*scale
                out[:,t*TILE:(t+1)*TILE]=z.astype(BF)

def full(shape):
    return pl.BlockSpec(shape,lambda *a:(0,)*len(shape))
def params(mb): return pltpu.CompilerParams(vmem_limit_bytes=mb<<20)
sd=jax.ShapeDtypeStruct

def qkv_call(meta,x,w_own,w_par,b_own,b_par,vec):
    T,D=x.shape; half=w_own.shape[1]; inner=2*half
    ct,st=rope_tables(T)
    rows=lambda n:pl.BlockSpec((TB,n),lambda i,m:(i,0))
    return pl.pallas_call(qkv_kernel,
        out_shape=(sd((T,D),BF),sd((T,inner),BF),sd((T,inner),BF),sd((T,inner),BF),sd((T,TILE),F32),sd((T,TILE),F32),sd((3,inner,D),BF)),
        grid_spec=pltpu.PrefetchScalarGridSpec(num_scalar_prefetch=1,grid=(T//TB,),
            in_specs=[rows(D),full(w_own.shape),full(w_par.shape),full(b_own.shape),full(b_par.shape),full(vec.shape),full((T,TILE)),full((T,TILE))],
            out_specs=(rows(D),rows(inner),rows(inner),rows(inner),rows(TILE),rows(TILE),full((3,inner,D))),
            scratch_shapes=[pltpu.VMEM((8,inner),F32)]),
        compiler_params=params(44),
        cost_estimate=pl.CostEstimate(flops=2*T*D*3*inner,bytes_accessed=12<<20,transcendentals=0),
        name="norm_qkv_rope")(meta,x,w_own,w_par,b_own,b_par,vec,jnp.asarray(ct),jnp.asarray(st))

def gelu_parts(h):
    cdf=0.5*(1.0+lax.erf(h*(1.0/math.sqrt(2.0))))
    return h*cdf, cdf+h*jnp.exp(-0.5*h*h)*(1.0/math.sqrt(2.0*math.pi))

FC=256
def ffn_kernel(meta,mix_ref,x_ref,og_ref,tg_ref,woo_ref,wop_ref,vec_ref,wuo_ref,wup_ref,buo_ref,bup_ref,wdo_ref,wdp_ref,
               n2_ref,dl_ref,ao_ref,ap_ref,uo_ref,up_ref,mid_ref,wo_ref,sbo_ref,sbp_ref):
    i=pl.program_id(0)
    @pl.when(i==0)
    def _():
        weave(wo_ref,woo_ref,wop_ref)
        sbo_ref[...]=jnp.zeros_like(sbo_ref); sbp_ref[...]=jnp.zeros_like(sbp_ref)
    live=meta[9]
    mid=x_ref[...].astype(F32)+nn(mix_ref[...],wo_ref[...])+vec_ref[2:3,:]
    mid_ref[...]=mid
    nrm,r=ln_stats(mid)
    n2=(nrm*vec_ref[3:4,:]+vec_ref[4:5,:]).astype(BF)
    n2_ref[...]=n2
    at=lax.broadcasted_iota(jnp.int32,(8,TB),1)+i*TB
    keep=jnp.where((tg_ref[...]>=0)&(at<live),1.0,0.0)
    dl=(og_ref[...].astype(F32)*keep.T[:,0:1]).astype(BF)
    dl_ref[...]=dl
    for wu,bu,wd,a_ref,u_ref,sb in ((wuo_ref,buo_ref,wdo_ref,ao_ref,uo_ref,sbo_ref),(wup_ref,bup_ref,wdp_ref,ap_ref,up_ref,sbp_ref)):
        for c in range(0,wu.shape[1],FC):
            h=nn(n2,wu[:,c:c+FC])+bu[:,c:c+FC]
            ag=nt(dl,wd[c:c+FC,:])
            val,slope=gelu_parts(h)
            a_ref[:,c:c+FC]=val.astype(BF)
            hg=ag*slope
            u_ref[:,c:c+FC]=hg.astype(BF)
            sb[0:1,c:c+FC]+=jnp.sum(hg,axis=0,keepdims=True)

def ffn_call(meta,mixed,x,og,targets,wo_own,wo_par,vec,wu_own,wu_par,bu_own,bu_par,wd_own,wd_par):
    T,D=x.shape; inner=mixed.shape[1]; fh=wu_own.shape[1]
    rows=lambda n:pl.BlockSpec((TB,n),lambda i,m:(i,0))
    return pl.pallas_call(ffn_kernel,
        out_shape=(sd((T,D),BF),sd((T,D),BF),sd((T,fh),BF),sd((T,fh),BF),sd((T,fh),BF),sd((T,fh),BF),sd((T,D),F32),sd((inner,D),BF),
                   sd((8,fh),F32),sd((8,fh),F32)),
        grid_spec=pltpu.PrefetchScalarGridSpec(num_scalar_prefetch=1,grid=(T//TB,),
            in_specs=[rows(inner),rows(D),rows(D),pl.BlockSpec((1,TB),lambda i,m:(0,i)),full(wo_own.shape),full(wo_par.shape),full(vec.shape),
                      full(wu_own.shape),full(wu_par.shape),full(bu_own.shape),full(bu_par.shape),full(wd_own.shape),full(wd_par.shape)],
            out_specs=(rows(D),rows(D),rows(fh),rows(fh),rows(fh),rows(fh),rows(D),full((inner,D)),full((8,fh)),full((8,fh)))),
        compiler_params=params(48),
        cost_estimate=pl.CostEstimate(flops=2*T*D*(inner+4*fh),bytes_accessed=22<<20,transcendentals=0),
        name="mix_and_ffn_in")(meta,mixed,x,og,targets,wo_own,wo_par,vec,wu_own,wu_par,bu_own,bu_par,wd_own,wd_par)

def mid_kernel(meta,ao_ref,ap_ref,uo_ref,up_ref,mid_ref,og_ref,tg_ref,vec_ref,wuo_ref,wup_ref,wdo_ref,wdp_ref,wo_ref,out_ref,mg_ref,bl_ref,xg_ref,sum_ref):
    i=pl.program_id(0)
    @pl.when(i==0)
    def _():
        sum_ref[...]=jnp.zeros_like(sum_ref)
    live=meta[9]
    at=lax.broadcasted_iota(jnp.int32,(8,TB),1)+i*TB
    keep=jnp.where((tg_ref[...]>=0)&(at<live),1.0,0.0)
    top=og_ref[...].astype(F32)*keep.T[:,0:1]
    sum_ref[3:4,:]+=jnp.sum(top,axis=0,keepdims=True)
    sg=nt(uo_ref[...],wuo_ref[...])+nt(up_ref[...],wup_ref[...])
    mid=mid_ref[...]
    nrm,r=ln_stats(mid)
    feed=nn(ao_ref[...],wdo_ref[...])+nn(ap_ref[...],wdp_ref[...])
    out_ref[...]=(mid+feed+vec_ref[5:6,:]).astype(BF)
    sum_ref[0:1,:]+=jnp.sum(sg*nrm,axis=0,keepdims=True)
    sum_ref[1:2,:]+=jnp.sum(sg,axis=0,keepdims=True)
    inner=sg*vec_ref[3:4,:]
    mg=top+r*(inner-jnp.mean(inner,axis=-1,keepdims=True)-nrm*jnp.mean(inner*nrm,axis=-1,keepdims=True))
    mg_ref[...]=mg
    sum_ref[2:3,:]+=jnp.sum(mg,axis=0,keepdims=True)
    bl=mg.astype(BF)
    bl_ref[...]=bl
    xg_ref[...]=nt(bl,wo_ref[...]).astype(BF)

def mid_call(meta,ao,ap,uo,up,mid,og,targets,vec,wu_own,wu_par,wd_own,wd_par,wo):
    T,D=mid.shape; inner=wo.shape[0]; fh=ao.shape[1]
    rows=lambda n:pl.BlockSpec((TB,n),lambda i,m:(i,0))
    return pl.pallas_call(mid_kernel,
        out_shape=(sd((T,D),BF),sd((T,D),F32),sd((T,D),BF),sd((T,inner),BF),sd((8,D),F32)),
        grid_spec=pltpu.PrefetchScalarGridSpec(num_scalar_prefetch=1,grid=(T//TB,),
            in_specs=[rows(fh)]*4+[rows(D),rows(D),pl.BlockSpec((1,TB),lambda i,m:(0,i)),full(vec.shape),full(wu_own.shape),full(wu_par.shape),full(wd_own.shape),full(wd_par.shape),full(wo.shape)],
            out_specs=(rows(D),rows(D),rows(D),rows(inner),full((8,D)))),
        compiler_params=params(48),
        cost_estimate=pl.CostEstimate(flops=2*T*D*(inner+4*fh),bytes_accessed=28<<20,transcendentals=0),
        name="ffn_out_and_norm_grad")(meta,ao,ap,uo,up,mid,og,targets,vec,wu_own,wu_par,wd_own,wd_par,wo)

SLOTS=16
GC=640
def ffn_grads_kernel(at,n_ref,dl_ref,ao_ref,ap_ref,uo_ref,up_ref,own_ref,par_ref,nT):
    i=pl.program_id(0)
    @pl.when(i==0)
    def _():
        nT[...]=n_ref[...].T
    r=n_ref.shape[1]//SLOTS; rd=own_ref.shape[1]//2
    per=GC//rd
    for u_ref,a_ref,g_ref,m in ((uo_ref,ao_ref,own_ref,at[0]),(up_ref,ap_ref,par_ref,at[1])):
        g=nn(nT[...],u_ref[...])
        for step in range(rd//r):
            @pl.when(i==step)
            def _(step=step,g=g,g_ref=g_ref,m=m):
                for s in range(SLOTS):
                    g_ref[s^m,step*r:(step+1)*r,:]=g[s*r:(s+1)*r].astype(BF)
        g=tn(a_ref[...],dl_ref[...])
        for s in range(per):
            g_ref[(i*per+s)^m,rd:2*rd,:]=g[s*rd:(s+1)*rd].astype(BF)

def ffn_grads_call(at,n2,dl,ao,ap,uo,up):
    T,D=n2.shape; fh=ao.shape[1]
    cols=pl.BlockSpec((T,GC),lambda i,m:(0,i))
    shape=(SLOTS,2*fh//SLOTS,D)
    return pl.pallas_call(ffn_grads_kernel,
        out_shape=(sd(shape,BF),)*2,
        grid_spec=pltpu.PrefetchScalarGridSpec(num_scalar_prefetch=1,grid=(fh//GC,),
            in_specs=[full((T,D)),full((T,D)),cols,cols,cols,cols],
            out_specs=(full(shape),)*2,
            scratch_shapes=[pltpu.VMEM((D,T),BF)]),
        compiler_params=params(52),
        cost_estimate=pl.CostEstimate(flops=2*T*D*4*fh,bytes_accessed=24<<20,transcendentals=0),
        name="ffn_weight_grads")(at,n2,dl,ao,ap,uo,up)

def in_grad_kernel(dq_ref,dk_ref,dv_ref,w_ref,x_ref,mg_ref,g_ref,out_ref,sum_ref):
    i=pl.program_id(0)
    @pl.when(i==0)
    def _():
        sum_ref[...]=jnp.zeros_like(sum_ref)
    fg=nn(dq_ref[...],w_ref[0])+nn(dk_ref[...],w_ref[1])+nn(dv_ref[...],w_ref[2])
    nrm,r=ln_stats(x_ref[...].astype(F32))
    sum_ref[0:1,:]+=jnp.sum(fg*nrm,axis=0,keepdims=True)
    sum_ref[1:2,:]+=jnp.sum(fg,axis=0,keepdims=True)
    inner=fg*g_ref[0:1,:]
    out_ref[...]=(mg_ref[...]+r*(inner-jnp.mean(inner,axis=-1,keepdims=True)-nrm*jnp.mean(inner*nrm,axis=-1,keepdims=True))).astype(BF)

def in_grad_call(dq,dk,dv,wc,x,mg,g):
    T,D=x.shape; inner=dq.shape[1]
    rows=lambda n:pl.BlockSpec((TB,n),lambda i:(i,0))
    return pl.pallas_call(in_grad_kernel,
        out_shape=(sd((T,D),BF),sd((8,D),F32)),grid=(T//TB,),
        in_specs=[rows(inner)]*3+[full(wc.shape),rows(D),rows(D),full(g.shape)],
        out_specs=(rows(D),full((8,D))),
        compiler_params=params(40),
        cost_estimate=pl.CostEstimate(flops=6*T*D*inner,bytes_accessed=14<<20,transcendentals=0),
        name="input_grad")(dq,dk,dv,wc,x,mg,g)

def put(ref,m,flat,val):
    rows=ref.shape[1]
    a=0; n=val.shape[0]
    while a<n:
        s,off=divmod(flat+a,rows)
        step=min(rows-off,n-a)
        ref[s^m,off:off+step,:]=val[a:a+step].astype(ref.dtype)
        a+=step

def take(ref,m,flat,out,scale):
    rows=ref.shape[1]
    a=0; n=out.shape[0]
    while a<n:
        s,off=divmod(flat+a,rows)
        step=min(rows-off,n-a)
        out[a:a+step,:]=ref[s^m,off:off+step,:].astype(F32)*scale
        a+=step

def attn_grads_kernel(extra,at,n_ref,dq_ref,dk_ref,dv_ref,*rest):
    if extra:
        bl_ref,mix_ref,own_ref,par_ref=rest
    else:
        own_ref,par_ref=rest
    m=at[0]
    tiles=dq_ref.shape[1]//TILE
    for c,l in enumerate((dq_ref,dk_ref,dv_ref)):
        g=tn(l[...],n_ref[...])
        for t in range(tiles):
            flat=(t*3+c)*HALF
            put(own_ref,m,flat,g[t*TILE:t*TILE+HALF]); put(par_ref,at[1],flat,g[t*TILE+HALF:(t+1)*TILE])
    if extra:
        g=tn(mix_ref[...],bl_ref[...])
        for t in range(g.shape[0]//TILE):
            flat=(tiles*3+t)*HALF
            put(own_ref,m,flat,g[t*TILE:t*TILE+HALF]); put(par_ref,at[1],flat,g[t*TILE+HALF:(t+1)*TILE])

def attn_grads_call(at,n1,dq,dk,dv,begin,count,extra):
    T,D=n1.shape; inner=dq.shape[1]
    w=TILE
    cols=pl.BlockSpec((T,count*w),lambda i,m:(0,begin//count)) if begin%count==0 else None
    if cols is None:
        cols=pl.BlockSpec((pl.Element(T),pl.Element(count*w)),lambda i,m:(0,begin*w))
    rows=(3*count*HALF+(inner//2 if extra else 0))//SLOTS
    more=[full((T,D)),full((T,inner))] if extra else []
    return pl.pallas_call(functools.partial(attn_grads_kernel,bool(extra)),
        out_shape=(sd((SLOTS,rows,D),BF),)*2,
        grid_spec=pltpu.PrefetchScalarGridSpec(num_scalar_prefetch=1,grid=(1,),
            in_specs=[full((T,D)),cols,cols,cols]+more,
            out_specs=(full((SLOTS,rows,D)),)*2),
        compiler_params=params(40),
        cost_estimate=pl.CostEstimate(flops=2*T*D*(3*count*w+(inner if extra else 0)),bytes_accessed=8<<20,transcendentals=0),
        name="attention_weight_grads")(at,n1,dq,dk,dv,*extra)

def scale_kernel(at,f_ref,a_ref,o_ref,p_ref):
    f=f_ref[0,0]; m=at[0]
    rd=a_ref.shape[1]//2; r=o_ref.shape[0]//SLOTS; w=a_ref.shape[2]
    for s in range(SLOTS):
        for step in range(rd//r):
            o_ref[s*r:(s+1)*r,step*w:(step+1)*w]=a_ref[s^m,step*r:(step+1)*r,:].astype(F32)*f
        p_ref[s*rd:(s+1)*rd,:]=a_ref[s^m,rd:2*rd,:].astype(F32)*f

def scale_call(at,factor,a,D,fh):
    return pl.pallas_call(scale_kernel,out_shape=(sd((D,fh),F32),sd((fh,D),F32)),
        grid_spec=pltpu.PrefetchScalarGridSpec(num_scalar_prefetch=1,grid=(1,),
            in_specs=[pl.BlockSpec(memory_space=pltpu.SMEM),full(a.shape)],
            out_specs=(full((D,fh)),full((fh,D)))),
        compiler_params=params(32),
        cost_estimate=pl.CostEstimate(flops=0,bytes_accessed=10<<20,transcendentals=0),
        name="scale_ffn_grads")(at,factor,a)

def scale_attn_kernel(at,f_ref,a_ref,b_ref,o_ref,p_ref):
    f=f_ref[0,0]
    tiles=o_ref.shape[1]//HALF
    first=(a_ref.shape[0]*a_ref.shape[1]-p_ref.shape[0])//(3*HALF)
    for t in range(tiles):
        for c in range(3):
            out=o_ref.at[c,t*HALF:(t+1)*HALF,:]
            if t<first: take(a_ref,at[0],(t*3+c)*HALF,out,f)
            else: take(b_ref,at[0],((t-first)*3+c)*HALF,out,f)
    take(a_ref,at[0],first*3*HALF,p_ref,f)

def scale_attn_call(at,factor,a,b,half,D):
    return pl.pallas_call(scale_attn_kernel,out_shape=(sd((3,half,D),F32),sd((half,D),F32)),
        grid_spec=pltpu.PrefetchScalarGridSpec(num_scalar_prefetch=1,grid=(1,),
            in_specs=[pl.BlockSpec(memory_space=pltpu.SMEM),full(a.shape),full(b.shape)],
            out_specs=(full((3,half,D)),full((half,D)))),
        compiler_params=params(32),
        cost_estimate=pl.CostEstimate(flops=0,bytes_accessed=5<<20,transcendentals=0),
        name="scale_attention_grads")(at,factor,a,b)


def swap_cores(a):
    return lax.ppermute(a,"tensor",[(0,1),(1,0)])

def across(a,bits):
    n=lax.axis_size("dp")
    return lax.ppermute(a,("dp","tensor"),[(2*i+c,2*(i^(1<<bits[c]))+c) for i in range(n) for c in range(2)])

def plus(a,b):
    return (a.astype(F32)+b.astype(F32)).astype(BF)

def bit_orders():
    bits=lax.axis_size("dp").bit_length()-1
    line=list(range(bits))
    other=[1,2,3,0]+line[4:]
    return list(zip(line,other))

def slot_offset(order,core):
    me=lax.axis_index("dp")
    out=jnp.int32(0)
    for i in range(4):
        bit=jnp.where(core==0,order[i][0],order[i][1])
        out=out|(((me>>bit)&1)<<(3-i))
    return out

def add_halves(keep,got):
    n=keep.shape[0]//2
    return plus(keep[:n],got[:n]),plus(keep[n:],got[n:])

class Lane:
    def __init__(self,own,par,order):
        self.own=own; self.order=order
        self.step=0
        self.got=swap_cores(par)
    def land(self,got):
        order=self.order; rest=len(order)-4
        step=self.step
        if step==0:
            self.low,self.high=add_halves(self.own,got)
        elif step<=3:
            self.low,self.high=add_halves(self.low,got)
        elif step<=4+rest:
            self.low=plus(self.low,got)
        else:
            self.low=jnp.concatenate([self.low,got],axis=0)
        self.step=step=step+1
        if step<=4:
            self.got=across(self.high,order[step-1])
        elif step<=4+rest:
            self.got=across(self.low,order[step-1])
        elif step<=8+rest:
            self.got=across(self.low,order[8+rest-step])
        else:
            self.got=None
    def finish(self):
        while self.got is not None:
            self.land(self.got)
        return self.low

def advance(token,*lanes):
    out=lax.optimization_barrier((token,)+tuple(l.got for l in lanes))
    for l,got in zip(lanes,out[1:]):
        l.land(got)
    return out[0]

def body(tokens,out_grad,segment_ids,token_live,live_rows,targets,predicted,w_qkv,b_qkv,w_out,b_out,
         norm1_gain,norm1_bias,norm2_gain,norm2_bias,w_up,b_up,w_down,b_down):
    member=lax.axis_index("tensor")
    x=tokens[0]; T,D=x.shape
    half=w_qkv.shape[2]; fh=w_up.shape[1]
    w_qkv=w_qkv.transpose(0,2,1)
    bias_own=jnp.concatenate([b_up,b_qkv.reshape(3*half)])
    bias_par=swap_cores(bias_own)
    w_qkv_p=swap_cores(w_qkv)
    lift=lambda a:a.astype(F32).reshape(1,-1)
    bias_own=lift(bias_own); bias_par=lift(bias_par)
    vec=jnp.concatenate([norm1_gain,norm1_bias,b_out,norm2_gain,norm2_bias,b_down]).astype(F32).reshape(6,D)
    w_out_p=swap_cores(w_out); w_up_p=swap_cores(w_up); w_down_p=swap_cores(w_down)
    segments=lax.dynamic_index_in_dim(segment_ids,member,0,keepdims=False)
    lived=lax.dynamic_index_in_dim(token_live,member,0,keepdims=False)
    starts=jnp.sum((segments[None,:]<jnp.arange(9,dtype=jnp.int32)[:,None]).astype(jnp.int32),axis=1)
    live=jnp.where(member<live_rows[0],jnp.sum(lived),0)
    meta=jnp.concatenate([starts,live[None],jnp.zeros((6,),jnp.int32)])
    order=bit_orders()
    at=jnp.stack([slot_offset(order,member),slot_offset(order,1-member)])
    n1,q,k,v,cos,sin,wc=qkv_call(meta,x,w_qkv,w_qkv_p,bias_own,bias_par,vec)
    mixed,lse=attend_fwd(meta,q,k,v)
    n2,dl,ao,ap,uo,up,mid,wo,sbo,sbp=ffn_call(meta,mixed,x,out_grad[0],targets,w_out,w_out_p,vec,
        w_up,w_up_p,bias_own,bias_par,w_down,w_down_p)
    gfo,gfp=ffn_grads_call(at,n2,dl,ao,ap,uo,up)
    f_lane=Lane(gfo,gfp,order)
    turn,gfo=lax.optimization_barrier((meta,gfo))
    out_act,mg,bl,xg,sums=mid_call(turn,ao,ap,uo,up,mid,out_grad[0],targets,vec,w_up,w_up_p,w_down,w_down_p,wo)
    xg,turn=lax.optimization_barrier((xg,turn))
    turn=advance(turn,f_lane)
    held=None
    def attend(t):
        nonlocal held,turn
        held=attend_bwd(turn,q,k,v,mixed,xg,lse,cos,sin,t,1,held)
        held0,turn=lax.optimization_barrier((held[0],turn))
        held=(held0,)+tuple(held[1:])
    attend(0); attend(1)
    turn=advance(turn,f_lane)
    attend(2)
    turn=advance(turn,f_lane)
    gco,gcp=attn_grads_call(at,n1,held[0],held[1],held[2],0,3,(bl,mixed))
    c_lane=Lane(gco,gcp,order)
    attend(3)
    turn=advance(turn,f_lane,c_lane)
    attend(4)
    turn=advance(turn,f_lane,c_lane)
    dq,dk,dv,psum3=held
    gdo,gdp=attn_grads_call(at,n1,dq,dk,dv,3,2,())
    d_lane=Lane(gdo,gdp,order)
    dq,turn,gdo=lax.optimization_barrier((dq,turn,gdo))
    in_grad,sums1=in_grad_call(dq,dk,dv,wc,x,mg,vec)
    in_grad,turn=lax.optimization_barrier((in_grad,turn))
    turn=advance(turn,f_lane,c_lane,d_lane)
    turn=advance(turn,f_lane,c_lane,d_lane)
    sums1,turn,d_lane.low=lax.optimization_barrier((sums1,turn,d_lane.low))
    gf=f_lane.finish(); gc=c_lane.finish(); ge=d_lane.finish()
    masked=(targets[0]>=0)&(jnp.arange(T)<live)
    correct=masked&(predicted[0]==targets[0])
    row_correct=jnp.sum(correct.astype(jnp.int32))[None]
    tallies=jnp.stack([live.astype(F32),jnp.sum(masked.astype(F32)),row_correct[0].astype(F32)])
    own=jnp.concatenate([psum3[:,0:3,:HALF].transpose(1,0,2).reshape(-1),sbo[0]])
    par=jnp.concatenate([psum3[:,0:3,HALF:].transpose(1,0,2).reshape(-1),sbp[0]])
    shared=jnp.concatenate([sums[2],sums[3],sums1[0],sums1[1],sums[0],sums[1],tallies,jnp.zeros((-(3*half+fh+6*D+3)%TILE,),F32)])
    small=jnp.concatenate([own,shared]).reshape(-1,TILE)
    other=jnp.concatenate([par,shared]).reshape(-1,TILE)
    small=small+swap_cores(other)
    n=lax.axis_size("dp")
    for bits in order:
        small=small+across(small,bits)
    small=small.reshape(-1)
    base=3*half+fh
    totals=small[base+6*D:base+6*D+3]
    factor=n/totals[1]
    part=lambda i:small[base+i*D:base+(i+1)*D]*factor
    f=factor.reshape(1,1)
    s_up,s_down=scale_call(at,f,gf,D,fh); s_qkv,s_out=scale_attn_call(at,f,gc,ge,half,D)
    return (out_act[None],in_grad[None],s_qkv.transpose(0,2,1),small[:3*half].reshape(3,half)*factor,s_out,part(0),
            part(2),part(3),part(4),part(5),s_up,small[3*half:base]*factor,s_down,part(1),
            totals.astype(jnp.int32),row_correct)


def solution(mesh):
    in_specs = (
        P(("dp", "tensor"), None, None),
        P(("dp", "tensor"), None, None),
        P("dp", None),
        P("dp", None),
        P("dp"),
        P(("dp", "tensor"), None),
        P(("dp", "tensor"), None),
        P(None, None, "tensor"),
        P(None, "tensor"),
        P("tensor", None),
        P(),
        P(),
        P(),
        P(),
        P(),
        P(None, "tensor"),
        P("tensor"),
        P("tensor", None),
        P(),
    )
    out_specs = (
        P(("dp", "tensor"), None, None),
        P(("dp", "tensor"), None, None),
        P(None, None, "tensor"),
        P(None, "tensor"),
        P("tensor", None),
        P(),
        P(),
        P(),
        P(),
        P(),
        P(None, "tensor"),
        P("tensor"),
        P("tensor", None),
        P(),
        P(),
        P(("dp", "tensor")),
    )
    return jax.shard_map(body, mesh=mesh, in_specs=in_specs, out_specs=out_specs, check_vma=False)
```

```python
import functools, math
import numpy as np
import jax, jax.numpy as jnp
from jax import lax
from jax.experimental import pallas as pl
from jax.experimental.pallas import tpu as pltpu
from jax.sharding import PartitionSpec as P
BF=jnp.bfloat16; F32=jnp.float32
QB=256; CH=128; TILE=128; HD=32; NEG=-1e9

def nn(a,b): return lax.dot_general(a,b,(((1,),(0,)),((),())),preferred_element_type=F32)
def nt(a,b): return lax.dot_general(a,b,(((1,),(1,)),((),())),preferred_element_type=F32)
def tn(a,b): return lax.dot_general(a,b,(((0,),(0,)),((),())),preferred_element_type=F32)

def seg_start(meta,idx):
    out=jnp.zeros_like(idx)
    for s in range(1,8):
        out=jnp.where(idx>=meta[s],meta[s],out)
    return out

def key_range(meta,first,length,backward):
    live=meta[9]
    lo=jnp.int32(0); hi=jnp.int32(length)
    for s in range(1,8):
        lo=jnp.where(meta[s]<=first,meta[s],lo)
    for s in range(7,0,-1):
        hi=jnp.where(meta[s]>first+QB-1,meta[s],hi)
    if backward:
        hi=jnp.minimum(hi,live)
    else:
        hi=jnp.minimum(hi,jnp.maximum(live,first+QB))
        lo=jnp.where(lo>=live,first,lo)
    k0=lax.div(lo,CH)*CH
    span=jnp.maximum(lax.div(hi+CH-1,CH)*CH-k0,2*CH)
    k0=jnp.minimum(k0,length-span)
    return pl.multiple_of(k0,CH),span

def query_span(meta,first,qn):
    live=meta[9]
    qi=lax.broadcasted_iota(jnp.int32,(8,qn),1)+first
    lo=jnp.zeros_like(qi); hi=jnp.full_like(qi,meta[8])
    for s in range(1,8):
        lo=jnp.where(qi>=meta[s],meta[s],lo)
    for s in range(7,0,-1):
        hi=jnp.where(qi<meta[s],meta[s],hi)
    return qi,lo,jnp.minimum(hi,live)

def bias_rows(spans,k0,rows,diagonal):
    qi,lo,hi=spans
    ki=lax.broadcasted_iota(jnp.int32,qi.shape,0)+k0
    out=[]
    for r in range(0,rows,8):
        at=ki+r
        ok=(at>=lo)&(at<hi)
        if diagonal: ok=ok|(at==qi)
        out.append(jnp.where(ok,0.0,NEG))
    return jnp.concatenate(out,axis=0)

RCX=256
PAIR=1
def chunks(w):
    return [(c,min(RCX,w-c)) for c in range(0,w,RCX)]
def fwd_kernel(meta,q_ref,k_ref,v_ref,o_ref,lse_ref,vt,bias,sbuf,pbuf):
    length=k_ref.shape[0]
    vt[...]=v_ref[...].T
    lane=lax.broadcasted_iota(jnp.int32,(QB,TILE),1)
    lax.fori_loop(0,length//QB,lambda qb,_:fwd_block(qb,meta,q_ref,k_ref,o_ref,lse_ref,vt,bias,sbuf,pbuf,lane,length),0)

def fwd_block(qb,meta,q_ref,k_ref,o_ref,lse_ref,vt,bias,sbuf,pbuf,lane,length):
    first=pl.multiple_of(qb*QB,QB)
    k0,span=key_range(meta,first,length,False)
    nh=TILE//HD
    for w in range(2*CH,length+1,CH):
        @pl.when(span==w)
        def _(w=w):
            spans=query_span(meta,first,QB)
            for c,RC in chunks(w):
                bias[c:c+RC,:]=bias_rows(spans,k0+c,RC,True)
            q=q_ref[pl.ds(first,QB),:]
            outs=[]
            def scores(h):
                qm=jnp.where(lax.div(lane,HD)==h,q,jnp.zeros_like(q))
                top=None
                for c,RC in chunks(w):
                    s=nt(k_ref[pl.ds(k0+c,RC),:],qm)+bias[c:c+RC,:]
                    sbuf[h%2,c:c+RC,:]=s
                    t=jnp.max(s.reshape(RC//8,8,QB),axis=0)
                    top=t if top is None else jnp.maximum(top,t)
                return jnp.max(top,axis=0,keepdims=True)
            def rest(h,m):
                tot=None
                for c,RC in chunks(w):
                    e=jnp.exp(sbuf[h%2,c:c+RC,:]-m)
                    t=jnp.sum(e.reshape(RC//8,8,QB),axis=0)
                    tot=t if tot is None else tot+t
                    pbuf[h%2,c:c+RC,:]=e.astype(BF)
                l=jnp.sum(tot,axis=0,keepdims=True)
                o=nn(vt[h*HD:(h+1)*HD,pl.ds(k0,w)],pbuf[h%2,0:w,:])
                outs.append(o/l)
                lse_ref[0,h:h+1,pl.ds(first,QB)]=m+jnp.log(l)
            ms=[scores(0)]
            for h in range(nh):
                if h+1<nh: ms.append(scores(h+1))
                rest(h,ms[h])
            o_ref[pl.ds(first,QB),:]=jnp.concatenate(outs,axis=0).T.astype(BF)
    return 0

def attend_fwd(meta,q,k,v):
    length,cols=q.shape
    tiles=cols//TILE
    return pl.pallas_call(fwd_kernel,
        out_shape=(jax.ShapeDtypeStruct((length,cols),BF),jax.ShapeDtypeStruct((tiles,TILE//HD,length),F32)),
        grid_spec=pltpu.PrefetchScalarGridSpec(num_scalar_prefetch=1,grid=(tiles,),
            in_specs=[pl.BlockSpec((length,TILE),lambda t,m:(0,t))]*3,
            out_specs=(pl.BlockSpec((length,TILE),lambda t,m:(0,t)),pl.BlockSpec((1,TILE//HD,length),lambda t,m:(t,0,0))),
            scratch_shapes=[pltpu.VMEM((TILE,length),BF),pltpu.VMEM((length,QB),F32),pltpu.VMEM((2,length,QB),F32),pltpu.VMEM((2,length,QB),BF)]),
        compiler_params=pltpu.CompilerParams(vmem_limit_bytes=20<<20),
        cost_estimate=pl.CostEstimate(flops=4*20*32*1024*1024,bytes_accessed=6<<20,transcendentals=0),
        name="attend_fwd")(meta,q,k,v)

def rope_back(x,cos,sin_b):
    y=x*sin_b
    lane=lax.broadcasted_iota(jnp.int32,x.shape,1)
    low=(lane & 16)==0
    return x*cos+jnp.where(low,pltpu.roll(y,TILE-16,1),-pltpu.roll(y,16,1))

def bwd_kernel(nin,meta,q_ref,k_ref,v_ref,o_ref,do_ref,lse_ref,cos_ref,sin_ref,*rest):
    dq_ref,dk_ref,dv_ref,sum_ref,tok_ref,kt,bias,pall,dsall,dkacc,dvacc=rest[nin:]
    tok_ref[...]=jnp.zeros_like(tok_ref)
    length=k_ref.shape[0]
    kt[...]=k_ref[...].T
    dkacc[...]=jnp.zeros_like(dkacc)
    dvacc[...]=jnp.zeros_like(dvacc)
    sum_ref[...]=jnp.zeros_like(sum_ref)
    lane=lax.broadcasted_iota(jnp.int32,(QB,TILE),1)
    def block(qb,_):
        bwd_block(qb,meta,q_ref,k_ref,v_ref,o_ref,do_ref,lse_ref,cos_ref,sin_ref,dq_ref,sum_ref,kt,bias,pall,dsall,dkacc,dvacc,lane,length)
        return 0
    lax.fori_loop(0,length//QB,block,0)
    dk=rope_back(dkacc[...],cos_ref[...],sin_ref[...])
    sum_ref[0,1:2,:]=jnp.sum(dk,axis=0,keepdims=True)
    dk_ref[...]=dk.astype(BF)
    dv=dvacc[...]
    sum_ref[0,2:3,:]=jnp.sum(dv,axis=0,keepdims=True)
    dv_ref[...]=dv.astype(BF)

def bwd_block(qb,meta,q_ref,k_ref,v_ref,o_ref,do_ref,lse_ref,cos_ref,sin_ref,dq_ref,sum_ref,kt,bias,pall,dsall,dkacc,dvacc,lane,length):
    first=pl.multiple_of(qb*QB,QB)
    nh=TILE//HD
    live=meta[9]
    k0,span=key_range(meta,first,length,True)
    @pl.when(first>=live)
    def _():
        dq_ref[pl.ds(first,QB),:]=jnp.zeros((QB,TILE),BF)
    for w in range(2*CH,length+1,CH):
        @pl.when((span==w)&(first<live))
        def _(w=w):
            spans=query_span(meta,first,QB)
            for c,RC in chunks(w):
                bias[c:c+RC,:]=bias_rows(spans,k0+c,RC,False)
            q=q_ref[pl.ds(first,QB),:]; do=do_ref[pl.ds(first,QB),:]
            x=do.astype(F32)*o_ref[pl.ds(first,QB),:].astype(F32)
            hi=x.astype(BF); lo=(x-hi.astype(F32)).astype(BF)
            pick=(lax.div(lax.broadcasted_iota(jnp.int32,(8,TILE),1),HD)==lax.broadcasted_iota(jnp.int32,(8,TILE),0))
            pick=jnp.where(pick,1.0,0.0).astype(BF)
            delta=nt(pick,hi)+nt(pick,lo)
            qms=[];dms=[];dqs=[]
            def scores(h):
                mine=lax.div(lane,HD)==h
                qm=jnp.where(mine,q,jnp.zeros_like(q)); dm=jnp.where(mine,do,jnp.zeros_like(do))
                qms.append(qm);dms.append(dm)
                lse_h=lse_ref[0,h:h+1,pl.ds(first,QB)]; del_h=delta[h:h+1,:]
                for c,RC in chunks(w):
                    p=jnp.exp(nt(k_ref[pl.ds(k0+c,RC),:],qm)+bias[c:c+RC,:]-lse_h)
                    pall[c:c+RC,h*QB:(h+1)*QB]=p.astype(BF)
                    ds=(p*(nt(v_ref[pl.ds(k0+c,RC),:],dm)-del_h)).astype(BF)
                    dsall[c:c+RC,h*QB:(h+1)*QB]=ds
            def grads(h):
                dqs.append(nn(kt[h*HD:(h+1)*HD,pl.ds(k0,w)],dsall[0:w,h*QB:(h+1)*QB]))
                if h%PAIR==PAIR-1:
                    lo=h+1-PAIR
                    for c,RC in chunks(w):
                        at=pl.ds(k0+c,RC)
                        dvacc[at,:]+=nn(pall[c:c+RC,lo*QB:(h+1)*QB],jnp.concatenate(dms[lo:h+1],axis=0))
                        dkacc[at,:]+=nn(dsall[c:c+RC,lo*QB:(h+1)*QB],jnp.concatenate(qms[lo:h+1],axis=0))
            for h in range(nh):
                scores(h)
                if h: grads(h-1)
            grads(nh-1)
            dq=jnp.concatenate(dqs,axis=0).T
            dq=rope_back(dq,cos_ref[pl.ds(first,QB),:],sin_ref[pl.ds(first,QB),:])*(1.0/math.sqrt(HD))
            sum_ref[0,0:1,:]+=jnp.sum(dq,axis=0,keepdims=True)
            dq_ref[pl.ds(first,QB),:]=dq.astype(BF)

def attend_bwd(meta,q,k,v,o,do,lse,cos,sin,begin,count,held,after=()):
    length,cols=q.shape
    tiles=cols//TILE
    col=pl.BlockSpec((length,TILE),lambda t,m:(0,begin+t)); tab=pl.BlockSpec((length,TILE),lambda t,m:(0,0))
    sd=jax.ShapeDtypeStruct
    held=() if held is None else tuple(held)
    return pl.pallas_call(functools.partial(bwd_kernel,len(held)+len(after)),
        out_shape=(sd((length,cols),BF),)*3+(sd((tiles,8,TILE),F32),sd((8,TILE),F32)),
        grid_spec=pltpu.PrefetchScalarGridSpec(num_scalar_prefetch=1,grid=(count,),
            in_specs=[col]*5+[pl.BlockSpec((1,TILE//HD,length),lambda t,m:(begin+t,0,0)),tab,tab]+[pl.BlockSpec(memory_space=pl.ANY)]*(len(held)+len(after)),
            out_specs=(col,col,col,pl.BlockSpec((1,8,TILE),lambda t,m:(begin+t,0,0)),pl.BlockSpec((8,TILE),lambda t,m:(0,0))),
            scratch_shapes=[pltpu.VMEM((TILE,length),BF),pltpu.VMEM((length,QB),F32),pltpu.VMEM((length,4*QB),BF),pltpu.VMEM((length,4*QB),BF),
                            pltpu.VMEM((length,TILE),F32),pltpu.VMEM((length,TILE),F32)]),
        input_output_aliases={9+i:i for i in range(len(held))},
        compiler_params=pltpu.CompilerParams(vmem_limit_bytes=22<<20),
        cost_estimate=pl.CostEstimate(flops=count*4*32*16*1024*1024,bytes_accessed=count*(2<<20),transcendentals=0),
        name="attend_bwd")(meta,q,k,v,o,do,lse,cos,sin,*held,*after)
EPS=1e-5
TB=256
HALF=TILE//2
def weave(out,own,par):
    for t in range(own.shape[0]//HALF):
        out[t*TILE:t*TILE+HALF,:]=own[t*HALF:(t+1)*HALF,:]
        out[t*TILE+HALF:(t+1)*TILE,:]=par[t*HALF:(t+1)*HALF,:]

def unweave(a):
    n=a.shape[0]//TILE
    return (jnp.concatenate([a[t*TILE:t*TILE+HALF] for t in range(n)],axis=0),
            jnp.concatenate([a[t*TILE+HALF:(t+1)*TILE] for t in range(n)],axis=0))

def ln_stats(x):
    mu=jnp.mean(x,axis=-1,keepdims=True)
    c=x-mu
    var=jnp.mean(c*c,axis=-1,keepdims=True)
    r=lax.rsqrt(var+EPS)
    return c*r,r

def rope_tables(length):
    lane=np.arange(TILE)%(HD//2)
    inv=np.exp(lane.astype(np.float64)*(-2.0*math.log(10000.0)/HD))
    ang=np.arange(length,dtype=np.float64)[:,None]*inv[None,:]
    return np.cos(ang).astype(np.float32),np.sin(ang).astype(np.float32)

def qkv_kernel(meta,x_ref,wo_ref,wp_ref,bo_ref,bp_ref,vec_ref,ct_ref,st_ref,n_ref,q_ref,k_ref,v_ref,cos_ref,sin_ref,wc_ref,b_ref):
    i=pl.program_id(0)
    @pl.when(i==0)
    def _():
        for c in range(3):
            weave(wc_ref.at[c],wo_ref.at[c],wp_ref.at[c])
            own=bo_ref[c:c+1,:].astype(F32); par=bp_ref[c:c+1,:].astype(F32)
            b_ref[c:c+1,:]=jnp.concatenate([r[:,t*HALF:(t+1)*HALF] for t in range(wo_ref.shape[1]//HALF) for r in (own,par)],axis=1)
    x=x_ref[...].astype(F32)
    nrm,_=ln_stats(x)
    n=(nrm*vec_ref[0:1,:]+vec_ref[1:2,:]).astype(BF)
    n_ref[...]=n
    first=i*TB
    top=ct_ref.shape[0]-1
    j=lax.broadcasted_iota(jnp.int32,(TB,TILE),0)+first
    cc=jnp.broadcast_to(ct_ref[0:1,:],(TB,TILE)); ss=jnp.broadcast_to(st_ref[0:1,:],(TB,TILE))
    for s in range(1,8):
        at=meta[s]; row=jnp.minimum(at,top)
        past=j>=at
        cc=jnp.where(past,ct_ref[pl.ds(row,1),:],cc)
        ss=jnp.where(past,st_ref[pl.ds(row,1),:],ss)
    cj=ct_ref[pl.ds(pl.multiple_of(first,TB),TB),:]; sj=st_ref[pl.ds(pl.multiple_of(first,TB),TB),:]
    cos=cj*cc+sj*ss; sin=sj*cc-cj*ss
    cos_ref[...]=cos; sin_ref[...]=sin
    low=(lax.broadcasted_iota(jnp.int32,(TB,TILE),1)&16)==0
    signed=jnp.where(low,-sin,sin)
    for c,(out,scale) in enumerate(((q_ref,1.0/math.sqrt(HD)),(k_ref,None),(v_ref,None))):
        p=nt(n,wc_ref[c])+b_ref[c:c+1,:]
        if c==2:
            out[...]=p.astype(BF)
        else:
            for t in range(p.shape[1]//TILE):
                y=p[:,t*TILE:(t+1)*TILE]
                z=y*cos+jnp.where(low,pltpu.roll(y,TILE-16,1),pltpu.roll(y,16,1))*signed
                if scale is not None: z=z*scale
                out[:,t*TILE:(t+1)*TILE]=z.astype(BF)

def full(shape):
    return pl.BlockSpec(shape,lambda *a:(0,)*len(shape))
def params(mb): return pltpu.CompilerParams(vmem_limit_bytes=mb<<20)
sd=jax.ShapeDtypeStruct

def qkv_call(meta,x,w_own,w_par,b_own,b_par,vec):
    T,D=x.shape; half=w_own.shape[1]; inner=2*half
    ct,st=rope_tables(T)
    rows=lambda n:pl.BlockSpec((TB,n),lambda i,m:(i,0))
    return pl.pallas_call(qkv_kernel,
        out_shape=(sd((T,D),BF),sd((T,inner),BF),sd((T,inner),BF),sd((T,inner),BF),sd((T,TILE),F32),sd((T,TILE),F32),sd((3,inner,D),BF)),
        grid_spec=pltpu.PrefetchScalarGridSpec(num_scalar_prefetch=1,grid=(T//TB,),
            in_specs=[rows(D),full(w_own.shape),full(w_par.shape),full(b_own.shape),full(b_par.shape),full(vec.shape),full((T,TILE)),full((T,TILE))],
            out_specs=(rows(D),rows(inner),rows(inner),rows(inner),rows(TILE),rows(TILE),full((3,inner,D))),
            scratch_shapes=[pltpu.VMEM((8,inner),F32)]),
        compiler_params=params(44),
        cost_estimate=pl.CostEstimate(flops=2*T*D*3*inner,bytes_accessed=12<<20,transcendentals=0),
        name="norm_qkv_rope")(meta,x,w_own,w_par,b_own,b_par,vec,jnp.asarray(ct),jnp.asarray(st))

def gelu_parts(h):
    cdf=0.5*(1.0+lax.erf(h*(1.0/math.sqrt(2.0))))
    return h*cdf, cdf+h*jnp.exp(-0.5*h*h)*(1.0/math.sqrt(2.0*math.pi))

FC=256
def ffn_kernel(meta,mix_ref,x_ref,og_ref,tg_ref,woo_ref,wop_ref,vec_ref,wuo_ref,wup_ref,bu_ref,wdo_ref,wdp_ref,
               n2_ref,dl_ref,ao_ref,ap_ref,uo_ref,up_ref,mid_ref,wo_ref,sbo_ref,sbp_ref):
    i=pl.program_id(0)
    @pl.when(i==0)
    def _():
        weave(wo_ref,woo_ref,wop_ref)
        sbo_ref[...]=jnp.zeros_like(sbo_ref); sbp_ref[...]=jnp.zeros_like(sbp_ref)
    live=meta[9]
    mid=x_ref[...].astype(F32)+nn(mix_ref[...],wo_ref[...])+vec_ref[2:3,:]
    mid_ref[...]=mid
    nrm,r=ln_stats(mid)
    n2=(nrm*vec_ref[3:4,:]+vec_ref[4:5,:]).astype(BF)
    n2_ref[...]=n2
    at=lax.broadcasted_iota(jnp.int32,(8,TB),1)+i*TB
    keep=jnp.where((tg_ref[...]>=0)&(at<live),1.0,0.0)
    dl=(og_ref[...].astype(F32)*keep.T[:,0:1]).astype(BF)
    dl_ref[...]=dl
    for wu,bu,wd,a_ref,u_ref,sb in ((wuo_ref,bu_ref.at[0:1],wdo_ref,ao_ref,uo_ref,sbo_ref),(wup_ref,bu_ref.at[1:2],wdp_ref,ap_ref,up_ref,sbp_ref)):
        for c in range(0,wu.shape[1],FC):
            h=nn(n2,wu[:,c:c+FC])+bu[:,c:c+FC]
            ag=nt(dl,wd[c:c+FC,:])
            val,slope=gelu_parts(h)
            a_ref[:,c:c+FC]=val.astype(BF)
            hg=ag*slope
            u_ref[:,c:c+FC]=hg.astype(BF)
            sb[0:1,c:c+FC]+=jnp.sum(hg,axis=0,keepdims=True)

def ffn_call(meta,mixed,x,og,targets,wo_own,wo_par,vec,wu_own,wu_par,bu,wd_own,wd_par):
    T,D=x.shape; inner=mixed.shape[1]; fh=wu_own.shape[1]
    rows=lambda n:pl.BlockSpec((TB,n),lambda i,m:(i,0))
    return pl.pallas_call(ffn_kernel,
        out_shape=(sd((T,D),BF),sd((T,D),BF),sd((T,fh),BF),sd((T,fh),BF),sd((T,fh),BF),sd((T,fh),BF),sd((T,D),F32),sd((inner,D),BF),
                   sd((8,fh),F32),sd((8,fh),F32)),
        grid_spec=pltpu.PrefetchScalarGridSpec(num_scalar_prefetch=1,grid=(T//TB,),
            in_specs=[rows(inner),rows(D),rows(D),pl.BlockSpec((1,TB),lambda i,m:(0,i)),full(wo_own.shape),full(wo_par.shape),full(vec.shape),
                      full(wu_own.shape),full(wu_par.shape),full(bu.shape),full(wd_own.shape),full(wd_par.shape)],
            out_specs=(rows(D),rows(D),rows(fh),rows(fh),rows(fh),rows(fh),rows(D),full((inner,D)),full((8,fh)),full((8,fh)))),
        compiler_params=params(48),
        cost_estimate=pl.CostEstimate(flops=2*T*D*(inner+4*fh),bytes_accessed=22<<20,transcendentals=0),
        name="mix_and_ffn_in")(meta,mixed,x,og,targets,wo_own,wo_par,vec,wu_own,wu_par,bu,wd_own,wd_par)

def mid_kernel(meta,ao_ref,ap_ref,uo_ref,up_ref,mid_ref,og_ref,tg_ref,vec_ref,wuo_ref,wup_ref,wdo_ref,wdp_ref,wo_ref,out_ref,mg_ref,bl_ref,xg_ref,sum_ref):
    i=pl.program_id(0)
    @pl.when(i==0)
    def _():
        sum_ref[...]=jnp.zeros_like(sum_ref)
    live=meta[9]
    at=lax.broadcasted_iota(jnp.int32,(8,TB),1)+i*TB
    keep=jnp.where((tg_ref[...]>=0)&(at<live),1.0,0.0)
    top=og_ref[...].astype(F32)*keep.T[:,0:1]
    sum_ref[3:4,:]+=jnp.sum(top,axis=0,keepdims=True)
    sg=nt(uo_ref[...],wuo_ref[...])+nt(up_ref[...],wup_ref[...])
    mid=mid_ref[...]
    nrm,r=ln_stats(mid)
    feed=nn(ao_ref[...],wdo_ref[...])+nn(ap_ref[...],wdp_ref[...])
    out_ref[...]=(mid+feed+vec_ref[5:6,:]).astype(BF)
    sum_ref[0:1,:]+=jnp.sum(sg*nrm,axis=0,keepdims=True)
    sum_ref[1:2,:]+=jnp.sum(sg,axis=0,keepdims=True)
    inner=sg*vec_ref[3:4,:]
    mg=top+r*(inner-jnp.mean(inner,axis=-1,keepdims=True)-nrm*jnp.mean(inner*nrm,axis=-1,keepdims=True))
    mg_ref[...]=mg
    sum_ref[2:3,:]+=jnp.sum(mg,axis=0,keepdims=True)
    bl=mg.astype(BF)
    bl_ref[...]=bl
    xg_ref[...]=nt(bl,wo_ref[...]).astype(BF)

def mid_call(meta,ao,ap,uo,up,mid,og,targets,vec,wu_own,wu_par,wd_own,wd_par,wo):
    T,D=mid.shape; inner=wo.shape[0]; fh=ao.shape[1]
    rows=lambda n:pl.BlockSpec((TB,n),lambda i,m:(i,0))
    return pl.pallas_call(mid_kernel,
        out_shape=(sd((T,D),BF),sd((T,D),F32),sd((T,D),BF),sd((T,inner),BF),sd((8,D),F32)),
        grid_spec=pltpu.PrefetchScalarGridSpec(num_scalar_prefetch=1,grid=(T//TB,),
            in_specs=[rows(fh)]*4+[rows(D),rows(D),pl.BlockSpec((1,TB),lambda i,m:(0,i)),full(vec.shape),full(wu_own.shape),full(wu_par.shape),full(wd_own.shape),full(wd_par.shape),full(wo.shape)],
            out_specs=(rows(D),rows(D),rows(D),rows(inner),full((8,D)))),
        compiler_params=params(48),
        cost_estimate=pl.CostEstimate(flops=2*T*D*(inner+4*fh),bytes_accessed=28<<20,transcendentals=0),
        name="ffn_out_and_norm_grad")(meta,ao,ap,uo,up,mid,og,targets,vec,wu_own,wu_par,wd_own,wd_par,wo)

SLOTS=16
GC=640
def ffn_grads_kernel(at,n_ref,dl_ref,ao_ref,ap_ref,uo_ref,up_ref,own_ref,par_ref,nT):
    i=pl.program_id(0)
    @pl.when(i==0)
    def _():
        nT[...]=n_ref[...].T
    r=n_ref.shape[1]//SLOTS; rd=own_ref.shape[1]//2
    per=GC//rd
    for u_ref,a_ref,g_ref,m in ((uo_ref,ao_ref,own_ref,at[0]),(up_ref,ap_ref,par_ref,at[1])):
        g=nn(nT[...],u_ref[...])
        for step in range(rd//r):
            @pl.when(i==step)
            def _(step=step,g=g,g_ref=g_ref,m=m):
                for s in range(SLOTS):
                    g_ref[s^m,step*r:(step+1)*r,:]=g[s*r:(s+1)*r].astype(BF)
        g=tn(a_ref[...],dl_ref[...])
        for s in range(per):
            g_ref[(i*per+s)^m,rd:2*rd,:]=g[s*rd:(s+1)*rd].astype(BF)

def ffn_grads_call(at,n2,dl,ao,ap,uo,up):
    T,D=n2.shape; fh=ao.shape[1]
    cols=pl.BlockSpec((T,GC),lambda i,m:(0,i))
    shape=(SLOTS,2*fh//SLOTS,D)
    return pl.pallas_call(ffn_grads_kernel,
        out_shape=(sd(shape,BF),)*2,
        grid_spec=pltpu.PrefetchScalarGridSpec(num_scalar_prefetch=1,grid=(fh//GC,),
            in_specs=[full((T,D)),full((T,D)),cols,cols,cols,cols],
            out_specs=(full(shape),)*2,
            scratch_shapes=[pltpu.VMEM((D,T),BF)]),
        compiler_params=params(52),
        cost_estimate=pl.CostEstimate(flops=2*T*D*4*fh,bytes_accessed=24<<20,transcendentals=0),
        name="ffn_weight_grads")(at,n2,dl,ao,ap,uo,up)

def in_grad_kernel(dq_ref,dk_ref,dv_ref,w_ref,x_ref,mg_ref,g_ref,*rest):
    out_ref,sum_ref=rest[-2:]
    i=pl.program_id(0)
    @pl.when(i==0)
    def _():
        sum_ref[...]=jnp.zeros_like(sum_ref)
    fg=nn(dq_ref[...],w_ref[0])+nn(dk_ref[...],w_ref[1])+nn(dv_ref[...],w_ref[2])
    nrm,r=ln_stats(x_ref[...].astype(F32))
    sum_ref[0:1,:]+=jnp.sum(fg*nrm,axis=0,keepdims=True)
    sum_ref[1:2,:]+=jnp.sum(fg,axis=0,keepdims=True)
    inner=fg*g_ref[0:1,:]
    out_ref[...]=(mg_ref[...]+r*(inner-jnp.mean(inner,axis=-1,keepdims=True)-nrm*jnp.mean(inner*nrm,axis=-1,keepdims=True))).astype(BF)

def in_grad_call(dq,dk,dv,wc,x,mg,g,after=()):
    T,D=x.shape; inner=dq.shape[1]
    rows=lambda n:pl.BlockSpec((TB,n),lambda i:(i,0))
    return pl.pallas_call(in_grad_kernel,
        out_shape=(sd((T,D),BF),sd((8,D),F32)),grid=(T//TB,),
        in_specs=[rows(inner)]*3+[full(wc.shape),rows(D),rows(D),full(g.shape)]+[pl.BlockSpec(memory_space=pl.ANY)]*len(after),
        out_specs=(rows(D),full((8,D))),
        compiler_params=params(40),
        cost_estimate=pl.CostEstimate(flops=6*T*D*inner,bytes_accessed=14<<20,transcendentals=0),
        name="input_grad")(dq,dk,dv,wc,x,mg,g,*after)

def put(ref,m,flat,val):
    rows=ref.shape[1]
    a=0; n=val.shape[0]
    while a<n:
        s,off=divmod(flat+a,rows)
        step=min(rows-off,n-a)
        ref[s^m,off:off+step,:]=val[a:a+step].astype(ref.dtype)
        a+=step

def take(ref,m,flat,out,scale):
    rows=ref.shape[1]
    a=0; n=out.shape[0]
    while a<n:
        s,off=divmod(flat+a,rows)
        step=min(rows-off,n-a)
        out[a:a+step,:]=ref[s^m,off:off+step,:].astype(F32)*scale
        a+=step

def attn_grads_kernel(extra,at,n_ref,dq_ref,dk_ref,dv_ref,*rest):
    own_ref,par_ref=rest[-2:]
    if extra: bl_ref,mix_ref=rest[:2]
    m=at[0]
    tiles=dq_ref.shape[1]//TILE
    for c,l in enumerate((dq_ref,dk_ref,dv_ref)):
        g=tn(l[...],n_ref[...])
        for t in range(tiles):
            flat=(t*3+c)*HALF
            put(own_ref,m,flat,g[t*TILE:t*TILE+HALF]); put(par_ref,at[1],flat,g[t*TILE+HALF:(t+1)*TILE])
    if extra:
        g=tn(mix_ref[...],bl_ref[...])
        for t in range(g.shape[0]//TILE):
            flat=(tiles*3+t)*HALF
            put(own_ref,m,flat,g[t*TILE:t*TILE+HALF]); put(par_ref,at[1],flat,g[t*TILE+HALF:(t+1)*TILE])

def attn_grads_call(at,n1,dq,dk,dv,begin,count,extra,after=()):
    T,D=n1.shape; inner=dq.shape[1]
    w=TILE
    cols=pl.BlockSpec((T,count*w),lambda i,m:(0,begin//count)) if begin%count==0 else None
    if cols is None:
        cols=pl.BlockSpec((pl.Element(T),pl.Element(count*w)),lambda i,m:(0,begin*w))
    rows=(3*count*HALF+(inner//2 if extra else 0))//SLOTS
    more=[full((T,D)),full((T,inner))] if extra else []
    return pl.pallas_call(functools.partial(attn_grads_kernel,bool(extra)),
        out_shape=(sd((SLOTS,rows,D),BF),)*2,
        grid_spec=pltpu.PrefetchScalarGridSpec(num_scalar_prefetch=1,grid=(1,),
            in_specs=[full((T,D)),cols,cols,cols]+more+[pl.BlockSpec(memory_space=pl.ANY)]*len(after),
            out_specs=(full((SLOTS,rows,D)),)*2),
        compiler_params=params(40),
        cost_estimate=pl.CostEstimate(flops=2*T*D*(3*count*w+(inner if extra else 0)),bytes_accessed=8<<20,transcendentals=0),
        name="attention_weight_grads")(at,n1,dq,dk,dv,*extra,*after)

def scale_kernel(at,f_ref,a_ref,o_ref,p_ref):
    f=f_ref[0,0]; m=at[0]
    rd=a_ref.shape[1]//2; r=o_ref.shape[0]//SLOTS; w=a_ref.shape[2]
    for s in range(SLOTS):
        for step in range(rd//r):
            o_ref[s*r:(s+1)*r,step*w:(step+1)*w]=a_ref[s^m,step*r:(step+1)*r,:].astype(F32)*f
        p_ref[s*rd:(s+1)*rd,:]=a_ref[s^m,rd:2*rd,:].astype(F32)*f

def scale_call(at,factor,a,D,fh):
    return pl.pallas_call(scale_kernel,out_shape=(sd((D,fh),F32),sd((fh,D),F32)),
        grid_spec=pltpu.PrefetchScalarGridSpec(num_scalar_prefetch=1,grid=(1,),
            in_specs=[pl.BlockSpec(memory_space=pltpu.SMEM),full(a.shape)],
            out_specs=(full((D,fh)),full((fh,D)))),
        compiler_params=params(32),
        cost_estimate=pl.CostEstimate(flops=0,bytes_accessed=10<<20,transcendentals=0),
        name="scale_ffn_grads")(at,factor,a)

def scale_attn_kernel(at,f_ref,a_ref,o_ref,p_ref):
    f=f_ref[0,0]
    tiles=o_ref.shape[1]//HALF
    for t in range(tiles):
        for c in range(3):
            take(a_ref,at[0],(t*3+c)*HALF,o_ref.at[c,t*HALF:(t+1)*HALF,:],f)
    take(a_ref,at[0],tiles*3*HALF,p_ref,f)

def scale_attn_call(at,factor,a,half,D):
    return pl.pallas_call(scale_attn_kernel,out_shape=(sd((3,half,D),F32),sd((half,D),F32)),
        grid_spec=pltpu.PrefetchScalarGridSpec(num_scalar_prefetch=1,grid=(1,),
            in_specs=[pl.BlockSpec(memory_space=pltpu.SMEM),full(a.shape)],
            out_specs=(full((3,half,D)),full((half,D)))),
        compiler_params=params(32),
        cost_estimate=pl.CostEstimate(flops=0,bytes_accessed=5<<20,transcendentals=0),
        name="scale_attention_grads")(at,factor,a)

def halves_kernel(a_ref,b_ref,c_ref,d_ref,*rest):
    low_ref,high_ref=rest[-2:]
    low_ref[...]=(a_ref[...].astype(F32)+b_ref[...].astype(F32)).astype(BF)
    high_ref[...]=(c_ref[...].astype(F32)+d_ref[...].astype(F32)).astype(BF)

def halves_call(keep,got,after):
    n,r,c=keep.shape; half=n//2; g=min(half,2); steps=half//g
    lo=pl.BlockSpec((g,r,c),lambda i:(i,0,0)); hi=pl.BlockSpec((g,r,c),lambda i:(steps+i,0,0))
    return pl.pallas_call(halves_kernel,out_shape=(sd((half,r,c),BF),)*2,grid=(steps,),
        in_specs=[lo,lo,hi,hi]+[pl.BlockSpec(memory_space=pl.ANY)]*len(after),out_specs=(lo,lo),
        compiler_params=params(24),
        cost_estimate=pl.CostEstimate(flops=0,bytes_accessed=6*n*r*c,transcendentals=0),
        name="add_slots")(keep,got,keep,got,*after)

def plus_kernel(a_ref,b_ref,*rest):
    rest[-1][...]=(a_ref[...].astype(F32)+b_ref[...].astype(F32)).astype(BF)

def plus_call(a,b,after):
    whole=pl.BlockSpec(a.shape,lambda i:(0,0,0))
    return pl.pallas_call(plus_kernel,out_shape=sd(a.shape,BF),grid=(1,),
        in_specs=[whole,whole]+[pl.BlockSpec(memory_space=pl.ANY)]*len(after),out_specs=whole,
        compiler_params=params(16),
        cost_estimate=pl.CostEstimate(flops=0,bytes_accessed=6*a.size,transcendentals=0),
        name="add_slot")(a,b,*after)


def swap_cores(a):
    return lax.ppermute(a,"tensor",[(0,1),(1,0)])

def across(a,bits):
    n=lax.axis_size("dp")
    return lax.ppermute(a,("dp","tensor"),[(2*i+c,2*(i^(1<<bits[c]))+c) for i in range(n) for c in range(2)])

def plus(a,b):
    return (a.astype(F32)+b.astype(F32)).astype(BF)

def bit_orders():
    bits=lax.axis_size("dp").bit_length()-1
    line=list(range(bits))
    other=[1,2,3,0]+line[4:]
    return list(zip(line,other))

def slot_offset(order,core):
    me=lax.axis_index("dp")
    out=jnp.int32(0)
    for i in range(4):
        bit=jnp.where(core==0,order[i][0],order[i][1])
        out=out|(((me>>bit)&1)<<(3-i))
    return out

def add_halves(keep,got):
    n=keep.shape[0]//2
    return plus(keep[:n],got[:n]),plus(keep[n:],got[n:])

class Lane:
    def __init__(self,own,par,order):
        self.own=own; self.order=order
        self.step=0
        self.got=swap_cores(par)
    def land(self,got,*after):
        order=self.order; rest=len(order)-4
        step=self.step
        if step==0:
            self.low,self.high=halves_call(self.own,got,after) if after else add_halves(self.own,got)
        elif step<=3:
            self.low,self.high=halves_call(self.low,got,after) if after else add_halves(self.low,got)
        elif step<=4+rest:
            self.low=plus_call(self.low,got,after) if after else plus(self.low,got)
        else:
            self.low=jnp.concatenate([self.low,got],axis=0)
        self.step=step=step+1
        if step<=4:
            self.got=across(self.high,order[step-1])
        elif step<=4+rest:
            self.got=across(self.low,order[step-1])
        elif step<=8+rest:
            self.got=across(self.low,order[8+rest-step])
        else:
            self.got=None
    def finish(self):
        while self.got is not None:
            self.land(self.got)
        return self.low

def advance(token,*lanes):
    out=lax.optimization_barrier((token,)+tuple(l.got for l in lanes))
    for l,got in zip(lanes,out[1:]):
        l.land(got)
    return out[0]

def settle(token,*lanes):
    out=lax.optimization_barrier((token,)+tuple(l.low for l in lanes))
    for l,low in zip(lanes,out[1:]):
        l.low=low
    return out[0]

def body(tokens,out_grad,segment_ids,token_live,live_rows,targets,predicted,w_qkv,b_qkv,w_out,b_out,
         norm1_gain,norm1_bias,norm2_gain,norm2_bias,w_up,b_up,w_down,b_down):
    member=lax.axis_index("tensor")
    x=tokens[0]; T,D=x.shape
    half=w_qkv.shape[2]; fh=w_up.shape[1]
    w_qkv=w_qkv.transpose(0,2,1)
    w_qkv_p=swap_cores(w_qkv)
    b_qkv_p=swap_cores(b_qkv)
    b_up_p=swap_cores(b_up)
    def rows(*parts):
        at=lax.broadcasted_iota(jnp.int32,(8,parts[0].shape[0]),0)
        out=jnp.zeros(at.shape,F32)
        for r,p in enumerate(parts):
            out=jnp.where(at==r,p.astype(F32)[None,:],out)
        return out
    vec=rows(norm1_gain,norm1_bias,b_out,norm2_gain,norm2_bias,b_down)
    b_up_rows=rows(b_up,b_up_p)
    w_out_p=swap_cores(w_out); w_up_p=swap_cores(w_up); w_down_p=swap_cores(w_down)
    segments=lax.dynamic_index_in_dim(segment_ids,member,0,keepdims=False)
    lived=lax.dynamic_index_in_dim(token_live,member,0,keepdims=False)
    starts=jnp.sum((segments[None,:]<jnp.arange(9,dtype=jnp.int32)[:,None]).astype(jnp.int32),axis=1)
    live=jnp.where(member<live_rows[0],jnp.sum(lived),0)
    meta=jnp.concatenate([starts,live[None],jnp.zeros((6,),jnp.int32)])
    order=bit_orders()
    at=jnp.stack([slot_offset(order,member),slot_offset(order,1-member)])
    n1,q,k,v,cos,sin,wc=qkv_call(meta,x,w_qkv,w_qkv_p,b_qkv,b_qkv_p,vec)
    mixed,lse=attend_fwd(meta,q,k,v)
    n2,dl,ao,ap,uo,up,mid,wo,sbo,sbp=ffn_call(meta,mixed,x,out_grad[0],targets,w_out,w_out_p,vec,
        w_up,w_up_p,b_up_rows,w_down,w_down_p)
    gfo,gfp=ffn_grads_call(at,n2,dl,ao,ap,uo,up)
    f_lane=Lane(gfo,gfp,order)
    turn,gfo=lax.optimization_barrier((meta,gfo))
    out_act,mg,bl,xg,sums=mid_call(turn,ao,ap,uo,up,mid,out_grad[0],targets,vec,w_up,w_up_p,w_down,w_down_p,wo)
    xg,turn=lax.optimization_barrier((xg,turn))
    f_lane.land(f_lane.got,xg)
    held=None
    token=None
    def attend(t):
        nonlocal held,token
        *held,token=attend_bwd(meta,q,k,v,mixed,xg,lse,cos,sin,t,1,held,(f_lane.low,) if token is None else (f_lane.low,token))
    attend(0); attend(1)
    f_lane.land(f_lane.got,token)
    attend(2)
    f_lane.land(f_lane.got,token)
    attend(3)
    f_lane.land(f_lane.got,token)
    attend(4)
    f_lane.land(f_lane.got,token)
    dq,dk,dv,psum3=held
    geo,gep=attn_grads_call(at,n1,dq,dk,dv,0,5,(bl,mixed),(f_lane.low,))
    e_lane=Lane(geo,gep,order)
    f_lane.land(f_lane.got)
    e_lane.land(e_lane.got)
    in_grad,sums1=in_grad_call(dq,dk,dv,wc,x,mg,vec,(e_lane.low,))
    gf=f_lane.finish(); ge=e_lane.finish()
    masked=(targets[0]>=0)&(jnp.arange(T)<live)
    correct=masked&(predicted[0]==targets[0])
    row_correct=jnp.sum(correct.astype(jnp.int32))[None]
    tallies=jnp.stack([live.astype(F32),jnp.sum(masked.astype(F32)),row_correct[0].astype(F32)])
    own=jnp.concatenate([psum3[:,0:3,:HALF].transpose(1,0,2).reshape(-1),sbo[0]])
    par=jnp.concatenate([psum3[:,0:3,HALF:].transpose(1,0,2).reshape(-1),sbp[0]])
    shared=jnp.concatenate([sums[2],sums[3],sums1[0],sums1[1],sums[0],sums[1],tallies,jnp.zeros((-(3*half+fh+6*D+3)%TILE,),F32)])
    small=jnp.concatenate([own,shared]).reshape(-1,TILE)
    other=jnp.concatenate([par,shared]).reshape(-1,TILE)
    small=small+swap_cores(other)
    n=lax.axis_size("dp")
    for bits in order:
        small=small+across(small,bits)
    small=small.reshape(-1)
    base=3*half+fh
    totals=small[base+6*D:base+6*D+3]
    factor=n/totals[1]
    part=lambda i:small[base+i*D:base+(i+1)*D]*factor
    f=factor.reshape(1,1)
    s_up,s_down=scale_call(at,f,gf,D,fh); s_qkv,s_out=scale_attn_call(at,f,ge,half,D)
    return (out_act[None],in_grad[None],s_qkv.transpose(0,2,1),small[:3*half].reshape(3,half)*factor,s_out,part(0),
            part(2),part(3),part(4),part(5),s_up,small[3*half:base]*factor,s_down,part(1),
            totals.astype(jnp.int32),row_correct)


def solution(mesh):
    in_specs = (
        P(("dp", "tensor"), None, None),
        P(("dp", "tensor"), None, None),
        P("dp", None),
        P("dp", None),
        P("dp"),
        P(("dp", "tensor"), None),
        P(("dp", "tensor"), None),
        P(None, None, "tensor"),
        P(None, "tensor"),
        P("tensor", None),
        P(),
        P(),
        P(),
        P(),
        P(),
        P(None, "tensor"),
        P("tensor"),
        P("tensor", None),
        P(),
    )
    out_specs = (
        P(("dp", "tensor"), None, None),
        P(("dp", "tensor"), None, None),
        P(None, None, "tensor"),
        P(None, "tensor"),
        P("tensor", None),
        P(),
        P(),
        P(),
        P(),
        P(),
        P(None, "tensor"),
        P("tensor"),
        P("tensor", None),
        P(),
        P(),
        P(("dp", "tensor")),
    )
    return jax.shard_map(body, mesh=mesh, in_specs=in_specs, out_specs=out_specs, check_vma=False)
```

```python
import functools, math
import numpy as np
import jax, jax.numpy as jnp
from jax import lax
from jax.experimental import pallas as pl
from jax.experimental.pallas import tpu as pltpu
from jax.sharding import PartitionSpec as P
BF=jnp.bfloat16; F32=jnp.float32
QB=256; CH=128; TILE=128; HD=32; NEG=-1e9

def nn(a,b): return lax.dot_general(a,b,(((1,),(0,)),((),())),preferred_element_type=F32)
def nt(a,b): return lax.dot_general(a,b,(((1,),(1,)),((),())),preferred_element_type=F32)
def tn(a,b): return lax.dot_general(a,b,(((0,),(0,)),((),())),preferred_element_type=F32)

def seg_start(meta,idx):
    out=jnp.zeros_like(idx)
    for s in range(1,8):
        out=jnp.where(idx>=meta[s],meta[s],out)
    return out

def key_range(meta,first,length,backward):
    live=meta[9]
    lo=jnp.int32(0); hi=jnp.int32(length)
    for s in range(1,8):
        lo=jnp.where(meta[s]<=first,meta[s],lo)
    for s in range(7,0,-1):
        hi=jnp.where(meta[s]>first+QB-1,meta[s],hi)
    if backward:
        hi=jnp.minimum(hi,live)
    else:
        hi=jnp.minimum(hi,jnp.maximum(live,first+QB))
        lo=jnp.where(lo>=live,first,lo)
    k0=lax.div(lo,CH)*CH
    span=jnp.maximum(lax.div(hi+CH-1,CH)*CH-k0,2*CH)
    k0=jnp.minimum(k0,length-span)
    return pl.multiple_of(k0,CH),span

def query_span(meta,first,qn):
    live=meta[9]
    qi=lax.broadcasted_iota(jnp.int32,(8,qn),1)+first
    lo=jnp.zeros_like(qi); hi=jnp.full_like(qi,meta[8])
    for s in range(1,8):
        lo=jnp.where(qi>=meta[s],meta[s],lo)
    for s in range(7,0,-1):
        hi=jnp.where(qi<meta[s],meta[s],hi)
    return qi,lo,jnp.minimum(hi,live)

def bias_rows(spans,k0,rows,diagonal):
    qi,lo,hi=spans
    ki=lax.broadcasted_iota(jnp.int32,qi.shape,0)+k0
    out=[]
    for r in range(0,rows,8):
        at=ki+r
        ok=(at>=lo)&(at<hi)
        if diagonal: ok=ok|(at==qi)
        out.append(jnp.where(ok,0.0,NEG))
    return jnp.concatenate(out,axis=0)

RCX=256
PAIR=1
def chunks(w):
    return [(c,min(RCX,w-c)) for c in range(0,w,RCX)]
def fwd_kernel(meta,q_ref,k_ref,v_ref,o_ref,lse_ref,vt,bias,sbuf,pbuf):
    length=k_ref.shape[0]
    vt[...]=v_ref[...].T
    lane=lax.broadcasted_iota(jnp.int32,(QB,TILE),1)
    lax.fori_loop(0,length//QB,lambda qb,_:fwd_block(qb,meta,q_ref,k_ref,o_ref,lse_ref,vt,bias,sbuf,pbuf,lane,length),0)

def fwd_block(qb,meta,q_ref,k_ref,o_ref,lse_ref,vt,bias,sbuf,pbuf,lane,length):
    first=pl.multiple_of(qb*QB,QB)
    k0,span=key_range(meta,first,length,False)
    nh=TILE//HD
    for w in range(2*CH,length+1,CH):
        @pl.when(span==w)
        def _(w=w):
            spans=query_span(meta,first,QB)
            for c,RC in chunks(w):
                bias[c:c+RC,:]=bias_rows(spans,k0+c,RC,True)
            q=q_ref[pl.ds(first,QB),:]
            outs=[]
            def scores(h):
                qm=jnp.where(lax.div(lane,HD)==h,q,jnp.zeros_like(q))
                top=None
                for c,RC in chunks(w):
                    s=nt(k_ref[pl.ds(k0+c,RC),:],qm)+bias[c:c+RC,:]
                    sbuf[h%2,c:c+RC,:]=s
                    t=jnp.max(s.reshape(RC//8,8,QB),axis=0)
                    top=t if top is None else jnp.maximum(top,t)
                return jnp.max(top,axis=0,keepdims=True)
            def rest(h,m):
                tot=None
                for c,RC in chunks(w):
                    e=jnp.exp(sbuf[h%2,c:c+RC,:]-m)
                    t=jnp.sum(e.reshape(RC//8,8,QB),axis=0)
                    tot=t if tot is None else tot+t
                    pbuf[h%2,c:c+RC,:]=e.astype(BF)
                l=jnp.sum(tot,axis=0,keepdims=True)
                o=nn(vt[h*HD:(h+1)*HD,pl.ds(k0,w)],pbuf[h%2,0:w,:])
                outs.append(o/l)
                lse_ref[0,h:h+1,pl.ds(first,QB)]=m+jnp.log(l)
            ms=[scores(0)]
            for h in range(nh):
                if h+1<nh: ms.append(scores(h+1))
                rest(h,ms[h])
            o_ref[pl.ds(first,QB),:]=jnp.concatenate(outs,axis=0).T.astype(BF)
    return 0

def attend_fwd(meta,q,k,v):
    length,cols=q.shape
    tiles=cols//TILE
    return pl.pallas_call(fwd_kernel,
        out_shape=(jax.ShapeDtypeStruct((length,cols),BF),jax.ShapeDtypeStruct((tiles,TILE//HD,length),F32)),
        grid_spec=pltpu.PrefetchScalarGridSpec(num_scalar_prefetch=1,grid=(tiles,),
            in_specs=[pl.BlockSpec((length,TILE),lambda t,m:(0,t))]*3,
            out_specs=(pl.BlockSpec((length,TILE),lambda t,m:(0,t)),pl.BlockSpec((1,TILE//HD,length),lambda t,m:(t,0,0))),
            scratch_shapes=[pltpu.VMEM((TILE,length),BF),pltpu.VMEM((length,QB),F32),pltpu.VMEM((2,length,QB),F32),pltpu.VMEM((2,length,QB),BF)]),
        compiler_params=pltpu.CompilerParams(vmem_limit_bytes=20<<20),
        cost_estimate=pl.CostEstimate(flops=4*20*32*1024*1024,bytes_accessed=6<<20,transcendentals=0),
        name="attend_fwd")(meta,q,k,v)

def rope_back(x,cos,sin_b):
    y=x*sin_b
    lane=lax.broadcasted_iota(jnp.int32,x.shape,1)
    low=(lane & 16)==0
    return x*cos+jnp.where(low,pltpu.roll(y,TILE-16,1),-pltpu.roll(y,16,1))

def bwd_kernel(nin,meta,q_ref,k_ref,v_ref,o_ref,do_ref,lse_ref,cos_ref,sin_ref,*rest):
    dq_ref,dk_ref,dv_ref,sum_ref,tok_ref,kt,bias,pall,dsall,dkacc,dvacc=rest[nin:]
    tok_ref[...]=jnp.zeros_like(tok_ref)
    length=k_ref.shape[0]
    kt[...]=k_ref[...].T
    dkacc[...]=jnp.zeros_like(dkacc)
    dvacc[...]=jnp.zeros_like(dvacc)
    sum_ref[...]=jnp.zeros_like(sum_ref)
    lane=lax.broadcasted_iota(jnp.int32,(QB,TILE),1)
    def block(qb,_):
        bwd_block(qb,meta,q_ref,k_ref,v_ref,o_ref,do_ref,lse_ref,cos_ref,sin_ref,dq_ref,sum_ref,kt,bias,pall,dsall,dkacc,dvacc,lane,length)
        return 0
    lax.fori_loop(0,length//QB,block,0)
    dk=rope_back(dkacc[...],cos_ref[...],sin_ref[...])
    sum_ref[0,1:2,:]=jnp.sum(dk,axis=0,keepdims=True)
    dk_ref[...]=dk.astype(BF)
    dv=dvacc[...]
    sum_ref[0,2:3,:]=jnp.sum(dv,axis=0,keepdims=True)
    dv_ref[...]=dv.astype(BF)

def bwd_block(qb,meta,q_ref,k_ref,v_ref,o_ref,do_ref,lse_ref,cos_ref,sin_ref,dq_ref,sum_ref,kt,bias,pall,dsall,dkacc,dvacc,lane,length):
    first=pl.multiple_of(qb*QB,QB)
    nh=TILE//HD
    live=meta[9]
    k0,span=key_range(meta,first,length,True)
    @pl.when(first>=live)
    def _():
        dq_ref[pl.ds(first,QB),:]=jnp.zeros((QB,TILE),BF)
    for w in range(2*CH,length+1,CH):
        @pl.when((span==w)&(first<live))
        def _(w=w):
            spans=query_span(meta,first,QB)
            for c,RC in chunks(w):
                bias[c:c+RC,:]=bias_rows(spans,k0+c,RC,False)
            q=q_ref[pl.ds(first,QB),:]; do=do_ref[pl.ds(first,QB),:]
            x=do.astype(F32)*o_ref[pl.ds(first,QB),:].astype(F32)
            hi=x.astype(BF); lo=(x-hi.astype(F32)).astype(BF)
            pick=(lax.div(lax.broadcasted_iota(jnp.int32,(8,TILE),1),HD)==lax.broadcasted_iota(jnp.int32,(8,TILE),0))
            pick=jnp.where(pick,1.0,0.0).astype(BF)
            delta=nt(pick,hi)+nt(pick,lo)
            qms=[];dms=[];dqs=[]
            def scores(h):
                mine=lax.div(lane,HD)==h
                qm=jnp.where(mine,q,jnp.zeros_like(q)); dm=jnp.where(mine,do,jnp.zeros_like(do))
                qms.append(qm);dms.append(dm)
                lse_h=lse_ref[0,h:h+1,pl.ds(first,QB)]; del_h=delta[h:h+1,:]
                for c,RC in chunks(w):
                    p=jnp.exp(nt(k_ref[pl.ds(k0+c,RC),:],qm)+bias[c:c+RC,:]-lse_h)
                    pall[c:c+RC,h*QB:(h+1)*QB]=p.astype(BF)
                    ds=(p*(nt(v_ref[pl.ds(k0+c,RC),:],dm)-del_h)).astype(BF)
                    dsall[c:c+RC,h*QB:(h+1)*QB]=ds
            def grads(h):
                dqs.append(nn(kt[h*HD:(h+1)*HD,pl.ds(k0,w)],dsall[0:w,h*QB:(h+1)*QB]))
                if h%PAIR==PAIR-1:
                    lo=h+1-PAIR
                    for c,RC in chunks(w):
                        at=pl.ds(k0+c,RC)
                        dvacc[at,:]+=nn(pall[c:c+RC,lo*QB:(h+1)*QB],jnp.concatenate(dms[lo:h+1],axis=0))
                        dkacc[at,:]+=nn(dsall[c:c+RC,lo*QB:(h+1)*QB],jnp.concatenate(qms[lo:h+1],axis=0))
            for h in range(nh):
                scores(h)
                if h: grads(h-1)
            grads(nh-1)
            dq=jnp.concatenate(dqs,axis=0).T
            dq=rope_back(dq,cos_ref[pl.ds(first,QB),:],sin_ref[pl.ds(first,QB),:])*(1.0/math.sqrt(HD))
            sum_ref[0,0:1,:]+=jnp.sum(dq,axis=0,keepdims=True)
            dq_ref[pl.ds(first,QB),:]=dq.astype(BF)

def attend_bwd(meta,q,k,v,o,do,lse,cos,sin,begin,count,held,after=()):
    length,cols=q.shape
    tiles=cols//TILE
    col=pl.BlockSpec((length,TILE),lambda t,m:(0,begin+t)); tab=pl.BlockSpec((length,TILE),lambda t,m:(0,0))
    sd=jax.ShapeDtypeStruct
    held=() if held is None else tuple(held)
    return pl.pallas_call(functools.partial(bwd_kernel,len(held)+len(after)),
        out_shape=(sd((length,cols),BF),)*3+(sd((tiles,8,TILE),F32),sd((8,TILE),F32)),
        grid_spec=pltpu.PrefetchScalarGridSpec(num_scalar_prefetch=1,grid=(count,),
            in_specs=[col]*5+[pl.BlockSpec((1,TILE//HD,length),lambda t,m:(begin+t,0,0)),tab,tab]+[pl.BlockSpec(memory_space=pl.ANY)]*(len(held)+len(after)),
            out_specs=(col,col,col,pl.BlockSpec((1,8,TILE),lambda t,m:(begin+t,0,0)),pl.BlockSpec((8,TILE),lambda t,m:(0,0))),
            scratch_shapes=[pltpu.VMEM((TILE,length),BF),pltpu.VMEM((length,QB),F32),pltpu.VMEM((length,4*QB),BF),pltpu.VMEM((length,4*QB),BF),
                            pltpu.VMEM((length,TILE),F32),pltpu.VMEM((length,TILE),F32)]),
        input_output_aliases={9+i:i for i in range(len(held))},
        compiler_params=pltpu.CompilerParams(vmem_limit_bytes=22<<20),
        cost_estimate=pl.CostEstimate(flops=count*4*32*16*1024*1024,bytes_accessed=count*(2<<20),transcendentals=0),
        name="attend_bwd")(meta,q,k,v,o,do,lse,cos,sin,*held,*after)
EPS=1e-5
TB=256
HALF=TILE//2
def weave(out,own,par):
    for t in range(own.shape[0]//HALF):
        out[t*TILE:t*TILE+HALF,:]=own[t*HALF:(t+1)*HALF,:]
        out[t*TILE+HALF:(t+1)*TILE,:]=par[t*HALF:(t+1)*HALF,:]

def unweave(a):
    n=a.shape[0]//TILE
    return (jnp.concatenate([a[t*TILE:t*TILE+HALF] for t in range(n)],axis=0),
            jnp.concatenate([a[t*TILE+HALF:(t+1)*TILE] for t in range(n)],axis=0))

def ln_stats(x):
    mu=jnp.mean(x,axis=-1,keepdims=True)
    c=x-mu
    var=jnp.mean(c*c,axis=-1,keepdims=True)
    r=lax.rsqrt(var+EPS)
    return c*r,r

def rope_tables(length):
    lane=np.arange(TILE)%(HD//2)
    inv=np.exp(lane.astype(np.float64)*(-2.0*math.log(10000.0)/HD))
    ang=np.arange(length,dtype=np.float64)[:,None]*inv[None,:]
    return np.cos(ang).astype(np.float32),np.sin(ang).astype(np.float32)

def qkv_kernel(meta,x_ref,wo_ref,wp_ref,bo_ref,bp_ref,vec_ref,ct_ref,st_ref,n_ref,q_ref,k_ref,v_ref,cos_ref,sin_ref,wc_ref,b_ref):
    i=pl.program_id(0)
    @pl.when(i==0)
    def _():
        for c in range(3):
            weave(wc_ref.at[c],wo_ref.at[c],wp_ref.at[c])
            own=bo_ref[c:c+1,:].astype(F32); par=bp_ref[c:c+1,:].astype(F32)
            b_ref[c:c+1,:]=jnp.concatenate([r[:,t*HALF:(t+1)*HALF] for t in range(wo_ref.shape[1]//HALF) for r in (own,par)],axis=1)
    x=x_ref[...].astype(F32)
    nrm,_=ln_stats(x)
    n=(nrm*vec_ref[0:1,:]+vec_ref[1:2,:]).astype(BF)
    n_ref[...]=n
    first=i*TB
    top=ct_ref.shape[0]-1
    j=lax.broadcasted_iota(jnp.int32,(TB,TILE),0)+first
    cc=jnp.broadcast_to(ct_ref[0:1,:],(TB,TILE)); ss=jnp.broadcast_to(st_ref[0:1,:],(TB,TILE))
    for s in range(1,8):
        at=meta[s]; row=jnp.minimum(at,top)
        past=j>=at
        cc=jnp.where(past,ct_ref[pl.ds(row,1),:],cc)
        ss=jnp.where(past,st_ref[pl.ds(row,1),:],ss)
    cj=ct_ref[pl.ds(pl.multiple_of(first,TB),TB),:]; sj=st_ref[pl.ds(pl.multiple_of(first,TB),TB),:]
    cos=cj*cc+sj*ss; sin=sj*cc-cj*ss
    cos_ref[...]=cos; sin_ref[...]=sin
    low=(lax.broadcasted_iota(jnp.int32,(TB,TILE),1)&16)==0
    signed=jnp.where(low,-sin,sin)
    for c,(out,scale) in enumerate(((q_ref,1.0/math.sqrt(HD)),(k_ref,None),(v_ref,None))):
        p=nt(n,wc_ref[c])+b_ref[c:c+1,:]
        if c==2:
            out[...]=p.astype(BF)
        else:
            for t in range(p.shape[1]//TILE):
                y=p[:,t*TILE:(t+1)*TILE]
                z=y*cos+jnp.where(low,pltpu.roll(y,TILE-16,1),pltpu.roll(y,16,1))*signed
                if scale is not None: z=z*scale
                out[:,t*TILE:(t+1)*TILE]=z.astype(BF)

def full(shape):
    return pl.BlockSpec(shape,lambda *a:(0,)*len(shape))
def params(mb): return pltpu.CompilerParams(vmem_limit_bytes=mb<<20)
sd=jax.ShapeDtypeStruct

def qkv_call(meta,x,w_own,w_par,b_own,b_par,vec):
    T,D=x.shape; half=w_own.shape[1]; inner=2*half
    ct,st=rope_tables(T)
    rows=lambda n:pl.BlockSpec((TB,n),lambda i,m:(i,0))
    return pl.pallas_call(qkv_kernel,
        out_shape=(sd((T,D),BF),sd((T,inner),BF),sd((T,inner),BF),sd((T,inner),BF),sd((T,TILE),F32),sd((T,TILE),F32),sd((3,inner,D),BF)),
        grid_spec=pltpu.PrefetchScalarGridSpec(num_scalar_prefetch=1,grid=(T//TB,),
            in_specs=[rows(D),full(w_own.shape),full(w_par.shape),full(b_own.shape),full(b_par.shape),full(vec.shape),full((T,TILE)),full((T,TILE))],
            out_specs=(rows(D),rows(inner),rows(inner),rows(inner),rows(TILE),rows(TILE),full((3,inner,D))),
            scratch_shapes=[pltpu.VMEM((8,inner),F32)]),
        compiler_params=params(44),
        cost_estimate=pl.CostEstimate(flops=2*T*D*3*inner,bytes_accessed=12<<20,transcendentals=0),
        name="norm_qkv_rope")(meta,x,w_own,w_par,b_own,b_par,vec,jnp.asarray(ct),jnp.asarray(st))

def gelu_parts(h):
    cdf=0.5*(1.0+lax.erf(h*(1.0/math.sqrt(2.0))))
    return h*cdf, cdf+h*jnp.exp(-0.5*h*h)*(1.0/math.sqrt(2.0*math.pi))

FC=256
def ffn_kernel(meta,mix_ref,x_ref,og_ref,tg_ref,woo_ref,wop_ref,vec_ref,wuo_ref,wup_ref,bu_ref,wdo_ref,wdp_ref,
               n2_ref,dl_ref,ao_ref,ap_ref,uo_ref,up_ref,mid_ref,wo_ref,sbo_ref,sbp_ref):
    i=pl.program_id(0)
    @pl.when(i==0)
    def _():
        weave(wo_ref,woo_ref,wop_ref)
        sbo_ref[...]=jnp.zeros_like(sbo_ref); sbp_ref[...]=jnp.zeros_like(sbp_ref)
    live=meta[9]
    mid=x_ref[...].astype(F32)+nn(mix_ref[...],wo_ref[...])+vec_ref[2:3,:]
    mid_ref[...]=mid
    nrm,r=ln_stats(mid)
    n2=(nrm*vec_ref[3:4,:]+vec_ref[4:5,:]).astype(BF)
    n2_ref[...]=n2
    at=lax.broadcasted_iota(jnp.int32,(8,TB),1)+i*TB
    keep=jnp.where((tg_ref[...]>=0)&(at<live),1.0,0.0)
    dl=(og_ref[...].astype(F32)*keep.T[:,0:1]).astype(BF)
    dl_ref[...]=dl
    for wu,bu,wd,a_ref,u_ref,sb in ((wuo_ref,bu_ref.at[0:1],wdo_ref,ao_ref,uo_ref,sbo_ref),(wup_ref,bu_ref.at[1:2],wdp_ref,ap_ref,up_ref,sbp_ref)):
        for c in range(0,wu.shape[1],FC):
            h=nn(n2,wu[:,c:c+FC])+bu[:,c:c+FC]
            ag=nt(dl,wd[c:c+FC,:])
            val,slope=gelu_parts(h)
            a_ref[:,c:c+FC]=val.astype(BF)
            hg=ag*slope
            u_ref[:,c:c+FC]=hg.astype(BF)
            sb[0:1,c:c+FC]+=jnp.sum(hg,axis=0,keepdims=True)

def ffn_call(meta,mixed,x,og,targets,wo_own,wo_par,vec,wu_own,wu_par,bu,wd_own,wd_par):
    T,D=x.shape; inner=mixed.shape[1]; fh=wu_own.shape[1]
    rows=lambda n:pl.BlockSpec((TB,n),lambda i,m:(i,0))
    return pl.pallas_call(ffn_kernel,
        out_shape=(sd((T,D),BF),sd((T,D),BF),sd((T,fh),BF),sd((T,fh),BF),sd((T,fh),BF),sd((T,fh),BF),sd((T,D),F32),sd((inner,D),BF),
                   sd((8,fh),F32),sd((8,fh),F32)),
        grid_spec=pltpu.PrefetchScalarGridSpec(num_scalar_prefetch=1,grid=(T//TB,),
            in_specs=[rows(inner),rows(D),rows(D),pl.BlockSpec((1,TB),lambda i,m:(0,i)),full(wo_own.shape),full(wo_par.shape),full(vec.shape),
                      full(wu_own.shape),full(wu_par.shape),full(bu.shape),full(wd_own.shape),full(wd_par.shape)],
            out_specs=(rows(D),rows(D),rows(fh),rows(fh),rows(fh),rows(fh),rows(D),full((inner,D)),full((8,fh)),full((8,fh)))),
        compiler_params=params(48),
        cost_estimate=pl.CostEstimate(flops=2*T*D*(inner+4*fh),bytes_accessed=22<<20,transcendentals=0),
        name="mix_and_ffn_in")(meta,mixed,x,og,targets,wo_own,wo_par,vec,wu_own,wu_par,bu,wd_own,wd_par)

def mid_kernel(meta,ao_ref,ap_ref,uo_ref,up_ref,mid_ref,og_ref,tg_ref,vec_ref,wuo_ref,wup_ref,wdo_ref,wdp_ref,wo_ref,out_ref,mg_ref,bl_ref,xg_ref,sum_ref):
    i=pl.program_id(0)
    @pl.when(i==0)
    def _():
        sum_ref[...]=jnp.zeros_like(sum_ref)
    live=meta[9]
    at=lax.broadcasted_iota(jnp.int32,(8,TB),1)+i*TB
    keep=jnp.where((tg_ref[...]>=0)&(at<live),1.0,0.0)
    top=og_ref[...].astype(F32)*keep.T[:,0:1]
    sum_ref[3:4,:]+=jnp.sum(top,axis=0,keepdims=True)
    sg=nt(uo_ref[...],wuo_ref[...])+nt(up_ref[...],wup_ref[...])
    mid=mid_ref[...]
    nrm,r=ln_stats(mid)
    feed=nn(ao_ref[...],wdo_ref[...])+nn(ap_ref[...],wdp_ref[...])
    out_ref[...]=(mid+feed+vec_ref[5:6,:]).astype(BF)
    sum_ref[0:1,:]+=jnp.sum(sg*nrm,axis=0,keepdims=True)
    sum_ref[1:2,:]+=jnp.sum(sg,axis=0,keepdims=True)
    inner=sg*vec_ref[3:4,:]
    mg=top+r*(inner-jnp.mean(inner,axis=-1,keepdims=True)-nrm*jnp.mean(inner*nrm,axis=-1,keepdims=True))
    mg_ref[...]=mg
    sum_ref[2:3,:]+=jnp.sum(mg,axis=0,keepdims=True)
    bl=mg.astype(BF)
    bl_ref[...]=bl
    xg_ref[...]=nt(bl,wo_ref[...]).astype(BF)

def mid_call(meta,ao,ap,uo,up,mid,og,targets,vec,wu_own,wu_par,wd_own,wd_par,wo):
    T,D=mid.shape; inner=wo.shape[0]; fh=ao.shape[1]
    rows=lambda n:pl.BlockSpec((TB,n),lambda i,m:(i,0))
    return pl.pallas_call(mid_kernel,
        out_shape=(sd((T,D),BF),sd((T,D),F32),sd((T,D),BF),sd((T,inner),BF),sd((8,D),F32)),
        grid_spec=pltpu.PrefetchScalarGridSpec(num_scalar_prefetch=1,grid=(T//TB,),
            in_specs=[rows(fh)]*4+[rows(D),rows(D),pl.BlockSpec((1,TB),lambda i,m:(0,i)),full(vec.shape),full(wu_own.shape),full(wu_par.shape),full(wd_own.shape),full(wd_par.shape),full(wo.shape)],
            out_specs=(rows(D),rows(D),rows(D),rows(inner),full((8,D)))),
        compiler_params=params(48),
        cost_estimate=pl.CostEstimate(flops=2*T*D*(inner+4*fh),bytes_accessed=28<<20,transcendentals=0),
        name="ffn_out_and_norm_grad")(meta,ao,ap,uo,up,mid,og,targets,vec,wu_own,wu_par,wd_own,wd_par,wo)

SLOTS=16
GC=640
def ffn_grads_kernel(at,n_ref,dl_ref,ao_ref,ap_ref,uo_ref,up_ref,own_ref,par_ref,nT):
    i=pl.program_id(0)
    @pl.when(i==0)
    def _():
        nT[...]=n_ref[...].T
    r=n_ref.shape[1]//SLOTS; rd=own_ref.shape[1]//2
    per=GC//rd
    for u_ref,a_ref,g_ref,m in ((uo_ref,ao_ref,own_ref,at[0]),(up_ref,ap_ref,par_ref,at[1])):
        g=nn(nT[...],u_ref[...])
        for step in range(rd//r):
            @pl.when(i==step)
            def _(step=step,g=g,g_ref=g_ref,m=m):
                for s in range(SLOTS):
                    g_ref[s^m,step*r:(step+1)*r,:]=g[s*r:(s+1)*r].astype(BF)
        g=tn(a_ref[...],dl_ref[...])
        for s in range(per):
            g_ref[(i*per+s)^m,rd:2*rd,:]=g[s*rd:(s+1)*rd].astype(BF)

def ffn_grads_call(at,n2,dl,ao,ap,uo,up):
    T,D=n2.shape; fh=ao.shape[1]
    cols=pl.BlockSpec((T,GC),lambda i,m:(0,i))
    shape=(SLOTS,2*fh//SLOTS,D)
    return pl.pallas_call(ffn_grads_kernel,
        out_shape=(sd(shape,BF),)*2,
        grid_spec=pltpu.PrefetchScalarGridSpec(num_scalar_prefetch=1,grid=(fh//GC,),
            in_specs=[full((T,D)),full((T,D)),cols,cols,cols,cols],
            out_specs=(full(shape),)*2,
            scratch_shapes=[pltpu.VMEM((D,T),BF)]),
        compiler_params=params(52),
        cost_estimate=pl.CostEstimate(flops=2*T*D*4*fh,bytes_accessed=24<<20,transcendentals=0),
        name="ffn_weight_grads")(at,n2,dl,ao,ap,uo,up)

def in_grad_kernel(dq_ref,dk_ref,dv_ref,w_ref,x_ref,mg_ref,g_ref,*rest):
    out_ref,sum_ref=rest[-2:]
    i=pl.program_id(0)
    @pl.when(i==0)
    def _():
        sum_ref[...]=jnp.zeros_like(sum_ref)
    fg=nn(dq_ref[...],w_ref[0])+nn(dk_ref[...],w_ref[1])+nn(dv_ref[...],w_ref[2])
    nrm,r=ln_stats(x_ref[...].astype(F32))
    sum_ref[0:1,:]+=jnp.sum(fg*nrm,axis=0,keepdims=True)
    sum_ref[1:2,:]+=jnp.sum(fg,axis=0,keepdims=True)
    inner=fg*g_ref[0:1,:]
    out_ref[...]=(mg_ref[...]+r*(inner-jnp.mean(inner,axis=-1,keepdims=True)-nrm*jnp.mean(inner*nrm,axis=-1,keepdims=True))).astype(BF)

def in_grad_call(dq,dk,dv,wc,x,mg,g,after=()):
    T,D=x.shape; inner=dq.shape[1]
    rows=lambda n:pl.BlockSpec((TB,n),lambda i:(i,0))
    return pl.pallas_call(in_grad_kernel,
        out_shape=(sd((T,D),BF),sd((8,D),F32)),grid=(T//TB,),
        in_specs=[rows(inner)]*3+[full(wc.shape),rows(D),rows(D),full(g.shape)]+[pl.BlockSpec(memory_space=pl.ANY)]*len(after),
        out_specs=(rows(D),full((8,D))),
        compiler_params=params(40),
        cost_estimate=pl.CostEstimate(flops=6*T*D*inner,bytes_accessed=14<<20,transcendentals=0),
        name="input_grad")(dq,dk,dv,wc,x,mg,g,*after)

def put(ref,m,flat,val):
    rows=ref.shape[1]
    a=0; n=val.shape[0]
    while a<n:
        s,off=divmod(flat+a,rows)
        step=min(rows-off,n-a)
        ref[s^m,off:off+step,:]=val[a:a+step].astype(ref.dtype)
        a+=step

def take(ref,m,flat,out,scale):
    rows=ref.shape[1]
    a=0; n=out.shape[0]
    while a<n:
        s,off=divmod(flat+a,rows)
        step=min(rows-off,n-a)
        out[a:a+step,:]=ref[s^m,off:off+step,:].astype(F32)*scale
        a+=step

def attn_grads_kernel(extra,at,n_ref,dq_ref,dk_ref,dv_ref,*rest):
    own_ref,par_ref=rest[-2:]
    if extra: bl_ref,mix_ref=rest[:2]
    m=at[0]
    tiles=dq_ref.shape[1]//TILE
    for c,l in enumerate((dq_ref,dk_ref,dv_ref)):
        g=tn(l[...],n_ref[...])
        for t in range(tiles):
            flat=(t*3+c)*HALF
            put(own_ref,m,flat,g[t*TILE:t*TILE+HALF]); put(par_ref,at[1],flat,g[t*TILE+HALF:(t+1)*TILE])
    if extra:
        g=tn(mix_ref[...],bl_ref[...])
        for t in range(g.shape[0]//TILE):
            flat=(tiles*3+t)*HALF
            put(own_ref,m,flat,g[t*TILE:t*TILE+HALF]); put(par_ref,at[1],flat,g[t*TILE+HALF:(t+1)*TILE])

def attn_grads_call(at,n1,dq,dk,dv,begin,count,extra,after=()):
    T,D=n1.shape; inner=dq.shape[1]
    w=TILE
    cols=pl.BlockSpec((T,count*w),lambda i,m:(0,begin//count)) if begin%count==0 else None
    if cols is None:
        cols=pl.BlockSpec((pl.Element(T),pl.Element(count*w)),lambda i,m:(0,begin*w))
    rows=(3*count*HALF+(inner//2 if extra else 0))//SLOTS
    more=[full((T,D)),full((T,inner))] if extra else []
    return pl.pallas_call(functools.partial(attn_grads_kernel,bool(extra)),
        out_shape=(sd((SLOTS,rows,D),BF),)*2,
        grid_spec=pltpu.PrefetchScalarGridSpec(num_scalar_prefetch=1,grid=(1,),
            in_specs=[full((T,D)),cols,cols,cols]+more+[pl.BlockSpec(memory_space=pl.ANY)]*len(after),
            out_specs=(full((SLOTS,rows,D)),)*2),
        compiler_params=params(40),
        cost_estimate=pl.CostEstimate(flops=2*T*D*(3*count*w+(inner if extra else 0)),bytes_accessed=8<<20,transcendentals=0),
        name="attention_weight_grads")(at,n1,dq,dk,dv,*extra,*after)

def scale_kernel(at,f_ref,a_ref,o_ref,p_ref):
    f=f_ref[0,0]; m=at[0]
    rd=a_ref.shape[1]//2; r=o_ref.shape[0]//SLOTS; w=a_ref.shape[2]
    for s in range(SLOTS):
        for step in range(rd//r):
            o_ref[s*r:(s+1)*r,step*w:(step+1)*w]=a_ref[s^m,step*r:(step+1)*r,:].astype(F32)*f
        p_ref[s*rd:(s+1)*rd,:]=a_ref[s^m,rd:2*rd,:].astype(F32)*f

def scale_call(at,factor,a,D,fh):
    return pl.pallas_call(scale_kernel,out_shape=(sd((D,fh),F32),sd((fh,D),F32)),
        grid_spec=pltpu.PrefetchScalarGridSpec(num_scalar_prefetch=1,grid=(1,),
            in_specs=[pl.BlockSpec(memory_space=pltpu.SMEM),full(a.shape)],
            out_specs=(full((D,fh)),full((fh,D)))),
        compiler_params=params(32),
        cost_estimate=pl.CostEstimate(flops=0,bytes_accessed=10<<20,transcendentals=0),
        name="scale_ffn_grads")(at,factor,a)

def scale_attn_kernel(at,f_ref,a_ref,o_ref,p_ref):
    f=f_ref[0,0]
    tiles=o_ref.shape[1]//HALF
    for t in range(tiles):
        for c in range(3):
            take(a_ref,at[0],(t*3+c)*HALF,o_ref.at[c,t*HALF:(t+1)*HALF,:],f)
    take(a_ref,at[0],tiles*3*HALF,p_ref,f)

def scale_attn_call(at,factor,a,half,D):
    return pl.pallas_call(scale_attn_kernel,out_shape=(sd((3,half,D),F32),sd((half,D),F32)),
        grid_spec=pltpu.PrefetchScalarGridSpec(num_scalar_prefetch=1,grid=(1,),
            in_specs=[pl.BlockSpec(memory_space=pltpu.SMEM),full(a.shape)],
            out_specs=(full((3,half,D)),full((half,D)))),
        compiler_params=params(32),
        cost_estimate=pl.CostEstimate(flops=0,bytes_accessed=5<<20,transcendentals=0),
        name="scale_attention_grads")(at,factor,a)

def halves_kernel(a_ref,b_ref,c_ref,d_ref,*rest):
    low_ref,high_ref=rest[-2:]
    low_ref[...]=(a_ref[...].astype(F32)+b_ref[...].astype(F32)).astype(BF)
    high_ref[...]=(c_ref[...].astype(F32)+d_ref[...].astype(F32)).astype(BF)

def halves_call(keep,got,after):
    n,r,c=keep.shape; half=n//2; g=min(half,2); steps=half//g
    lo=pl.BlockSpec((g,r,c),lambda i:(i,0,0)); hi=pl.BlockSpec((g,r,c),lambda i:(steps+i,0,0))
    return pl.pallas_call(halves_kernel,out_shape=(sd((half,r,c),BF),)*2,grid=(steps,),
        in_specs=[lo,lo,hi,hi]+[pl.BlockSpec(memory_space=pl.ANY)]*len(after),out_specs=(lo,lo),
        compiler_params=params(24),
        cost_estimate=pl.CostEstimate(flops=0,bytes_accessed=6*n*r*c,transcendentals=0),
        name="add_slots")(keep,got,keep,got,*after)

def plus_kernel(a_ref,b_ref,*rest):
    rest[-1][...]=(a_ref[...].astype(F32)+b_ref[...].astype(F32)).astype(BF)

def plus_call(a,b,after):
    whole=pl.BlockSpec(a.shape,lambda i:(0,0,0))
    return pl.pallas_call(plus_kernel,out_shape=sd(a.shape,BF),grid=(1,),
        in_specs=[whole,whole]+[pl.BlockSpec(memory_space=pl.ANY)]*len(after),out_specs=whole,
        compiler_params=params(16),
        cost_estimate=pl.CostEstimate(flops=0,bytes_accessed=6*a.size,transcendentals=0),
        name="add_slot")(a,b,*after)


def swap_cores(a):
    return lax.ppermute(a,"tensor",[(0,1),(1,0)])

def across(a,bits):
    n=lax.axis_size("dp")
    return lax.ppermute(a,("dp","tensor"),[(2*i+c,2*(i^(1<<bits[c]))+c) for i in range(n) for c in range(2)])

def plus(a,b):
    return (a.astype(F32)+b.astype(F32)).astype(BF)

def bit_orders():
    bits=lax.axis_size("dp").bit_length()-1
    line=list(range(bits))
    other=[1,2,3,0]+line[4:]
    return list(zip(line,other))

def slot_offset(order,core):
    me=lax.axis_index("dp")
    out=jnp.int32(0)
    for i in range(4):
        bit=jnp.where(core==0,order[i][0],order[i][1])
        out=out|(((me>>bit)&1)<<(3-i))
    return out

def add_halves(keep,got):
    n=keep.shape[0]//2
    return plus(keep[:n],got[:n]),plus(keep[n:],got[n:])

class Lane:
    def __init__(self,own,par,order):
        self.own=own; self.order=order
        self.step=0
        self.got=swap_cores(par)
    def land(self,got,*after):
        order=self.order; rest=len(order)-4
        step=self.step
        if step==0:
            self.low,self.high=halves_call(self.own,got,after) if after else add_halves(self.own,got)
        elif step<=3:
            self.low,self.high=halves_call(self.low,got,after) if after else add_halves(self.low,got)
        elif step<=4+rest:
            self.low=plus_call(self.low,got,after) if after else plus(self.low,got)
        else:
            self.low=jnp.concatenate([self.low,got],axis=0)
        self.step=step=step+1
        if step<=4:
            self.got=across(self.high,order[step-1])
        elif step<=4+rest:
            self.got=across(self.low,order[step-1])
        elif step<=8+rest:
            self.got=across(self.low,order[8+rest-step])
        else:
            self.got=None
    def finish(self):
        while self.got is not None:
            self.land(self.got)
        return self.low

def advance(token,*lanes):
    out=lax.optimization_barrier((token,)+tuple(l.got for l in lanes))
    for l,got in zip(lanes,out[1:]):
        l.land(got)
    return out[0]

def settle(token,*lanes):
    out=lax.optimization_barrier((token,)+tuple(l.low for l in lanes))
    for l,low in zip(lanes,out[1:]):
        l.low=low
    return out[0]

def body(tokens,out_grad,segment_ids,token_live,live_rows,targets,predicted,w_qkv,b_qkv,w_out,b_out,
         norm1_gain,norm1_bias,norm2_gain,norm2_bias,w_up,b_up,w_down,b_down):
    member=lax.axis_index("tensor")
    x=tokens[0]; T,D=x.shape
    half=w_qkv.shape[2]; fh=w_up.shape[1]
    w_qkv=w_qkv.transpose(0,2,1)
    w_qkv_p=swap_cores(w_qkv)
    b_qkv_p=swap_cores(b_qkv)
    b_up_p=swap_cores(b_up)
    def rows(*parts):
        at=lax.broadcasted_iota(jnp.int32,(8,parts[0].shape[0]),0)
        out=jnp.zeros(at.shape,F32)
        for r,p in enumerate(parts):
            out=jnp.where(at==r,p.astype(F32)[None,:],out)
        return out
    vec=rows(norm1_gain,norm1_bias,b_out,norm2_gain,norm2_bias,b_down)
    b_up_rows=rows(b_up,b_up_p)
    w_out_p=swap_cores(w_out); w_up_p=swap_cores(w_up); w_down_p=swap_cores(w_down)
    segments=lax.dynamic_index_in_dim(segment_ids,member,0,keepdims=False)
    lived=lax.dynamic_index_in_dim(token_live,member,0,keepdims=False)
    starts=jnp.sum((segments[None,:]<jnp.arange(9,dtype=jnp.int32)[:,None]).astype(jnp.int32),axis=1)
    live=jnp.where(member<live_rows[0],jnp.sum(lived),0)
    meta=jnp.concatenate([starts,live[None],jnp.zeros((6,),jnp.int32)])
    order=bit_orders()
    at=jnp.stack([slot_offset(order,member),slot_offset(order,1-member)])
    n1,q,k,v,cos,sin,wc=qkv_call(meta,x,w_qkv,w_qkv_p,b_qkv,b_qkv_p,vec)
    mixed,lse=attend_fwd(meta,q,k,v)
    n2,dl,ao,ap,uo,up,mid,wo,sbo,sbp=ffn_call(meta,mixed,x,out_grad[0],targets,w_out,w_out_p,vec,
        w_up,w_up_p,b_up_rows,w_down,w_down_p)
    gfo,gfp=ffn_grads_call(at,n2,dl,ao,ap,uo,up)
    f_lane=Lane(gfo,gfp,order)
    turn,gfo=lax.optimization_barrier((meta,gfo))
    out_act,mg,bl,xg,sums=mid_call(turn,ao,ap,uo,up,mid,out_grad[0],targets,vec,w_up,w_up_p,w_down,w_down_p,wo)
    xg,turn=lax.optimization_barrier((xg,turn))
    f_lane.land(f_lane.got,xg)
    held=None
    token=None
    def attend(t):
        nonlocal held,token
        *held,token=attend_bwd(meta,q,k,v,mixed,xg,lse,cos,sin,t,1,held,(f_lane.low,) if token is None else (f_lane.low,token))
    attend(0); attend(1)
    f_lane.land(f_lane.got,token)
    attend(2)
    f_lane.land(f_lane.got,token)
    attend(3)
    f_lane.land(f_lane.got,token)
    attend(4)
    f_lane.land(f_lane.got,token)
    dq,dk,dv,psum3=held
    geo,gep=attn_grads_call(at,n1,dq,dk,dv,0,5,(bl,mixed),(f_lane.low,))
    e_lane=Lane(geo,gep,order)
    f_lane.land(f_lane.got)
    e_lane.land(e_lane.got,f_lane.low)
    in_grad,sums1=in_grad_call(dq,dk,dv,wc,x,mg,vec,(e_lane.low,))
    gf=f_lane.finish(); ge=e_lane.finish()
    masked=(targets[0]>=0)&(jnp.arange(T)<live)
    correct=masked&(predicted[0]==targets[0])
    row_correct=jnp.sum(correct.astype(jnp.int32))[None]
    tallies=jnp.stack([live.astype(F32),jnp.sum(masked.astype(F32)),row_correct[0].astype(F32)])
    own=jnp.concatenate([psum3[:,0:3,:HALF].transpose(1,0,2).reshape(-1),sbo[0]])
    par=jnp.concatenate([psum3[:,0:3,HALF:].transpose(1,0,2).reshape(-1),sbp[0]])
    shared=jnp.concatenate([sums[2],sums[3],sums1[0],sums1[1],sums[0],sums[1],tallies,jnp.zeros((-(3*half+fh+6*D+3)%TILE,),F32)])
    small=jnp.concatenate([own,shared]).reshape(-1,TILE)
    other=jnp.concatenate([par,shared]).reshape(-1,TILE)
    small=small+swap_cores(other)
    n=lax.axis_size("dp")
    for bits in order:
        small=small+across(small,bits)
    small=small.reshape(-1)
    base=3*half+fh
    totals=small[base+6*D:base+6*D+3]
    factor=n/totals[1]
    part=lambda i:small[base+i*D:base+(i+1)*D]*factor
    f=factor.reshape(1,1)
    s_up,s_down=scale_call(at,f,gf,D,fh); s_qkv,s_out=scale_attn_call(at,f,ge,half,D)
    return (out_act[None],in_grad[None],s_qkv.transpose(0,2,1),small[:3*half].reshape(3,half)*factor,s_out,part(0),
            part(2),part(3),part(4),part(5),s_up,small[3*half:base]*factor,s_down,part(1),
            totals.astype(jnp.int32),row_correct)


def solution(mesh):
    in_specs = (
        P(("dp", "tensor"), None, None),
        P(("dp", "tensor"), None, None),
        P("dp", None),
        P("dp", None),
        P("dp"),
        P(("dp", "tensor"), None),
        P(("dp", "tensor"), None),
        P(None, None, "tensor"),
        P(None, "tensor"),
        P("tensor", None),
        P(),
        P(),
        P(),
        P(),
        P(),
        P(None, "tensor"),
        P("tensor"),
        P("tensor", None),
        P(),
    )
    out_specs = (
        P(("dp", "tensor"), None, None),
        P(("dp", "tensor"), None, None),
        P(None, None, "tensor"),
        P(None, "tensor"),
        P("tensor", None),
        P(),
        P(),
        P(),
        P(),
        P(),
        P(None, "tensor"),
        P("tensor"),
        P("tensor", None),
        P(),
        P(),
        P(("dp", "tensor")),
    )
    return jax.shard_map(body, mesh=mesh, in_specs=in_specs, out_specs=out_specs, check_vma=False)
```
